32 devices in a mesh: dp: 2 (over y), seq: 16 (over z, x, core).
Axes of the slice: x: 2, y: 2, z: 4, core: 2. Of those that a mesh axis runs over, the one named last changes fastest.
Arguments:
- layer_input: bfloat16 [4096, 1024], P(('dp', 'seq')), may hold values from -6 to 6
- norm_gain: bfloat16 [1024], P('dp'), may hold values from 0.5 to 1.5
- in_weight: bfloat16 [1024, 4384], P('dp'), may hold values from -0.1875 to 0.1875
- conv_weight: bfloat16 [4, 2304], P(None, 'dp'), may hold values from -3 to 3
- conv_bias: bfloat16 [2304], P('dp'), may hold values from -2 to 2
- step_bias: bfloat16 [32], P('dp'), may hold values from -5 to -1
- rate_log: bfloat16 [32], P('dp'), may hold values from -4 to 2
- skip_gain: bfloat16 [32], P('dp'), may hold values from 0.5 to 2
- gate_gain: bfloat16 [2048], P('dp'), may hold values from 0.5 to 1.5
- out_weight: bfloat16 [2048, 1024], P('dp'), may hold values from -0.125 to 0.125
- cotangent: bfloat16 [4096, 1024], P(('dp', 'seq')), may hold values from -6 to 6
Outputs:
- layer_output: bfloat16 [4096, 1024], P(('dp', 'seq'))
- input_grad: float32 [4096, 1024], P(('dp', 'seq'))
- norm_gain_grad: float32 [1024], P('dp')
- in_weight_grad: float32 [1024, 4384], P('dp')
- conv_weight_grad: float32 [4, 2304], P(None, 'dp')
- conv_bias_grad: float32 [2304], P('dp')
- step_bias_grad: float32 [32], P('dp')
- rate_log_grad: float32 [32], P('dp')
- skip_gain_grad: float32 [32], P('dp')
- gate_gain_grad: float32 [2048], P('dp')
- out_weight_grad: float32 [2048, 1024], P('dp')
The draws below stay inside these ranges and needn't reach their ends.
All inputs are finite; a program needn't handle non-finite values.
Results may differ from the reference program's by a relative error of at most 0.012.
Values may be sent and summed in bfloat16 or wider, within the bound.
No kernel may reach another device: no remote copies, remote signals or barrier semaphores. Data moves between devices by JAX's collectives and lax.ppermute only.
A program may use at most 192 MiB of HBM per device.

```python
import jax
import jax.numpy as jnp
from jax import lax

D = 1024
HEADS = 32
KCONV = 4
BLOCK = 256
DI = 2048
CONV_CH = 2304
PROJ = 4384
LEN = 2048
TOKENS = 4096
N_DP = 2


def level_of(key, dims, cuts, smallest, top_value):
    level, own = 1.0, jax.random.fold_in(key, 6)
    for position, parts in cuts:
        draws = jnp.exp(jax.random.uniform(jax.random.fold_in(own, position), (parts,), jnp.float32, smallest / len(cuts), top_value / len(cuts)))
        level = level * jnp.repeat(draws, dims[position] // parts).reshape([-1 if axis == position else 1 for axis in range(len(dims))])
    return level


def noise(key, shape, scale, most, pieces=(), kind=jnp.bfloat16):
    factor_of = level_of(key, shape, pieces, -0.22, 0.18) if pieces else 1.0
    array = jax.random.normal(key, shape, jnp.float32) * scale * factor_of
    return jnp.minimum(jnp.maximum(array, -most), most).astype(kind)


def setup_inputs(seed: int = 0) -> dict:
    streams_of = jax.random.split(jax.random.key(seed), 12)
    return {
        "layer_input": noise(streams_of[0], (TOKENS, D), 1.0, 6.0, ((0, 32),)),
        "norm_gain": jnp.clip(1.0 + 0.1 * jax.random.normal(streams_of[1], (D,), jnp.float32), 0.5, 1.5).astype(jnp.bfloat16),
        "in_weight": noise(streams_of[2], (D, PROJ), D ** -0.5, 0.1875, ((0, 2),)),
        "conv_weight": noise(streams_of[3], (KCONV, CONV_CH), KCONV ** -0.5, 3.0, ((1, 2),)),
        "conv_bias": noise(streams_of[4], (CONV_CH,), 0.4, 2.0, ((0, 2),)),
        "step_bias": jnp.clip(-5.0 + 4.0 * jax.random.uniform(streams_of[5], (HEADS,), jnp.float32) ** level_of(streams_of[5], (HEADS,), ((0, 2),), -0.2, 0.2), -5.0, -1.0).astype(jnp.bfloat16),
        "rate_log": jnp.clip(-4.0 + 6.0 * jax.random.uniform(streams_of[6], (HEADS,), jnp.float32) ** level_of(streams_of[6], (HEADS,), ((0, 2),), -0.2, 0.2), -4.0, 2.0).astype(jnp.bfloat16),
        "skip_gain": jnp.clip(0.5 + 1.5 * jax.random.uniform(streams_of[7], (HEADS,), jnp.float32) ** level_of(streams_of[7], (HEADS,), ((0, 2),), -0.2, 0.2), 0.5, 2.0).astype(jnp.bfloat16),
        "gate_gain": jnp.clip(1.0 + 0.1 * jax.random.normal(streams_of[8], (DI,), jnp.float32), 0.5, 1.5).astype(jnp.bfloat16),
        "out_weight": noise(streams_of[9], (DI, D), DI ** -0.5, 0.125, ((0, 2),)),
        "cotangent": noise(streams_of[10], (TOKENS, D), 1.0, 6.0, ((0, 32),)),
    }


@jax.custom_vjp
def low(v):
    return lax.optimization_barrier(v.astype(jnp.bfloat16)).astype(jnp.float32)

@jax.custom_vjp
def low_back(v):
    return v

def low_keep(v):
    return (low(v), None)

def low_pass(kept, grad):
    return (grad,)

def back_keep(v):
    return (v, None)

def back_low(kept, grad):
    return (low(grad),)
low.defvjp(low_keep, low_pass)
low_back.defvjp(back_keep, back_low)
epsilon = 1e-05
highest = lax.Precision.HIGHEST

def front_norm(values, gain):
    scale = lax.rsqrt(lax.optimization_barrier(jnp.mean(values * values, axis=-1, keepdims=True)) + epsilon)
    return values * scale * gain

def gated_norm(mixer_out, gate_in, gain):
    gated = mixer_out * jax.nn.silu(gate_in)
    scale = lax.rsqrt(lax.optimization_barrier(jnp.mean(gated * gated, axis=-1, keepdims=True)) + epsilon)
    return gated * scale * gain

def causal_conv(values, taps, offset):
    width = taps.shape[0]
    length = values.shape[0]
    padded = jnp.concatenate([jnp.zeros((width - 1, values.shape[1]), values.dtype), values], axis=0)
    total = offset[None, :] + jnp.zeros_like(values)
    for index in range(width):
        total = total + taps[index][None, :] * padded[index:index + length]
    return jax.nn.silu(total)

def scan_blocks(values, steps, rates, keys, queries):
    length, heads, hdim = values.shape
    states = keys.shape[1]
    blocks = length // BLOCK
    items = (values.reshape(blocks, BLOCK, heads, hdim), steps.reshape(blocks, BLOCK, heads), keys.reshape(blocks, BLOCK, states), queries.reshape(blocks, BLOCK, states))

    def one_block(state, item):
        val_blk, step_blk, key_blk, query_blk = item
        logs = (step_blk * rates[None, :]).T
        cums = jnp.cumsum(logs, axis=1)
        rows = lax.broadcasted_iota(jnp.int32, (BLOCK, BLOCK), 0)
        cols = lax.broadcasted_iota(jnp.int32, (BLOCK, BLOCK), 1)
        lower = (rows >= cols)[None]
        spread = cums[:, :, None] - cums[:, None, :]
        decay = jnp.where(lower, jnp.exp(jnp.where(lower, spread, 0.0)), 0.0)
        scores = jnp.dot(query_blk, key_blk.T, precision=highest)
        weights = scores[None] * decay * step_blk.T[:, None, :]
        inside = jnp.einsum('hts,shp->thp', weights, val_blk, precision=highest)
        carried = jnp.einsum('tn,hpn->thp', query_blk, state, precision=highest) * jnp.exp(cums).T[:, :, None]
        tail = jnp.exp(cums[:, -1:] - cums) * step_blk.T
        update = jnp.einsum('hs,shp,sn->hpn', tail, val_blk, key_blk, precision=highest)
        fresh = state * jnp.exp(cums[:, -1])[:, None, None] + update
        return (fresh, inside + carried)
    start = jnp.zeros((heads, hdim, states), jnp.float32)
    final_state, outputs = lax.scan(jax.checkpoint(one_block), start, items)
    return outputs.reshape(length, heads, hdim)

def mixer(x_head, step_raw, key_query, x_taps, x_offset, kq_taps, kq_offset, step_shift, rate_logs, skips):
    x_conv = causal_conv(x_head, x_taps, x_offset)
    kq_conv = causal_conv(key_query, kq_taps, kq_offset)
    states = kq_conv.shape[1] // 2
    keys = kq_conv[:, :states]
    queries = kq_conv[:, states:]
    steps = jax.nn.softplus(step_raw + step_shift[None, :])
    rates = -jnp.exp(rate_logs)
    heads = step_shift.shape[0]
    length = x_head.shape[0]
    values = x_conv.reshape(length, heads, -1)
    mixed = scan_blocks(values, steps, rates, keys, queries) + values * skips[None, :, None]
    return mixed.reshape(length, -1)

def layer(values, norm_gain, in_weight, conv_weight, conv_bias, step_bias, rate_log, skip_gain, gate_gain, out_weight):
    normed = low(front_norm(values, norm_gain))
    proj = low_back(low(jnp.dot(normed, in_weight, precision=highest)))
    gate_in = proj[:, :DI]
    x_part = proj[:, DI:2 * DI]
    kq_part = proj[:, 2 * DI:DI + CONV_CH]
    step_raw = proj[:, DI + CONV_CH:]
    mixed = mixer(x_part, step_raw, kq_part, conv_weight[:, :DI], conv_bias[:DI], conv_weight[:, DI:], conv_bias[DI:], step_bias, rate_log, skip_gain)
    mixer_out = low_back(low(mixed))
    normed_gate = low(gated_norm(mixer_out, gate_in, gate_gain))
    return values + jnp.dot(normed_gate, out_weight, precision=highest)

def reference(layer_input, norm_gain, in_weight, conv_weight, conv_bias, step_bias, rate_log, skip_gain, gate_gain, out_weight, cotangent):
    params = tuple((a.astype(jnp.float32) for a in (norm_gain, in_weight, conv_weight, conv_bias, step_bias, rate_log, skip_gain, gate_gain, out_weight)))
    sequences = layer_input.astype(jnp.float32).reshape(N_DP, LEN, D)
    cot_seqs = cotangent.astype(jnp.float32).reshape(N_DP, LEN, D)

    def one_sequence(totals, item):
        seq_vals, seq_cot = item
        result, pull = jax.vjp(layer, seq_vals, *params)
        grads = pull(seq_cot)
        sums = tuple((t + g for t, g in zip(totals, grads[1:])))
        return (sums, (result.astype(jnp.bfloat16), grads[0]))
    zeros = tuple((jnp.zeros_like(p) for p in params))
    totals, (results, in_grads) = lax.scan(one_sequence, zeros, (sequences, cot_seqs))
    return (results.reshape(TOKENS, D), in_grads.reshape(TOKENS, D), totals[0], totals[1], totals[2], totals[3], totals[4], totals[5], totals[6], totals[7], totals[8])
```

```python
import jax
import jax.numpy as jnp
from jax import lax
from jax.experimental import pallas as pl
from jax.experimental.pallas import tpu as pltpu
from jax.sharding import Mesh
from jax.sharding import PartitionSpec as P

BLOCK = 256
PRE = 16
LANES = 128
EPS = 1e-05
HIGHEST = lax.Precision.HIGHEST
F32 = jnp.float32
BF16 = jnp.bfloat16


def mm(a, b, da=1, db=0):
    return lax.dot_general(a, b, (((da,), (db,)), ((), ())), preferred_element_type=F32)


def mm_exact(a, b, da=1, db=0):
    return lax.dot_general(
        a, b, (((da,), (db,)), ((), ())), precision=HIGHEST, preferred_element_type=F32
    )


def iota(shape, dim):
    return lax.broadcasted_iota(jnp.int32, shape, dim)


def head_map(channels, hdim):
    return (jnp.right_shift(iota((LANES, channels), 1), hdim.bit_length() - 1) == iota((LANES, channels), 0)).astype(F32)


def unit(u):
    return u * lax.rsqrt(jnp.mean(u * u, axis=-1, keepdims=True) + EPS)


def sigmoid(v):
    return jax.nn.sigmoid(v)


def softplus(v):
    return jnp.maximum(v, 0.0) + jnp.log1p(jnp.exp(-jnp.abs(v)))


def masked(values, head, hdim):
    lanes = iota(values.shape, 1)
    own = (lanes >= head * hdim) & (lanes < (head + 1) * hdim)
    return jnp.where(own, values, jnp.zeros_like(values))


def front_kernel(hdim, x_ref, halo_ref, gain_ref, w_ref, cw_ref, cb_ref, sb_ref, rate_ref,
                 normed_ref, z_ref, raw_ref, pre_ref, xs_ref, kq_ref, dtb_ref, cums_ref,
                 stin_ref, cd_ref, fin_ref, dtot_ref, buf, st, cd):
    step_id = pl.program_id(0)
    ch = z_ref.shape[1]
    conv_ch = pre_ref.shape[1]
    gain = gain_ref[...]

    @pl.when(step_id == 0)
    def _():
        hn = (unit(halo_ref[...].astype(F32)) * gain).astype(BF16)
        hp = mm(hn, w_ref[:, ch : ch + conv_ch])
        buf[0:PRE, :] = hp.astype(BF16).astype(F32)
        st[...] = jnp.zeros_like(st)
        cd[...] = jnp.ones_like(cd)

    @pl.when(step_id > 0)
    def _():
        buf[0:PRE, :] = buf[BLOCK : BLOCK + PRE, :]

    normed = (unit(x_ref[...].astype(F32)) * gain).astype(BF16)
    normed_ref[...] = normed
    proj = mm(normed, w_ref[...])
    z_ref[...] = proj[:, :ch].astype(BF16)
    buf[PRE : PRE + BLOCK, :] = proj[:, ch : ch + conv_ch].astype(BF16).astype(F32)
    raw_ref[0] = buf[...].astype(BF16)
    pre = cb_ref[0:1, :] + cw_ref[0:1, :] * buf[PRE - 3 : PRE - 3 + BLOCK, :]
    for k in range(1, 4):
        pre = pre + cw_ref[k : k + 1, :] * buf[PRE - 3 + k : PRE - 3 + k + BLOCK, :]
    pre_ref[...] = pre
    act = pre * sigmoid(pre)
    dtb = proj[:, ch + conv_ch :].astype(BF16).astype(F32) + sb_ref[0:1, :]
    dtb_ref[...] = dtb
    step = softplus(dtb)
    logs = step * rate_ref[0:1, :]
    lower = (iota((BLOCK, BLOCK), 0) >= iota((BLOCK, BLOCK), 1)).astype(F32)
    cums = mm_exact(lower, logs)
    cums_ref[...] = cums
    hmap = head_map(ch, hdim)
    cums_b = mm_exact(cums, hmap)
    xs = act[:, :ch] * mm_exact(step, hmap)
    xs_ref[...] = xs.astype(BF16)
    kq = act[:, ch:].astype(BF16)
    kq_ref[...] = kq
    last = cums_b[BLOCK - 1 : BLOCK, :]
    tail = jnp.exp(last - cums_b)
    update = mm(kq[:, : kq.shape[1] // 2], (xs * tail).astype(BF16), 0, 0)
    stin_ref[0] = st[...]
    cd_ref[0] = cd[...]
    decay = jnp.exp(last)
    st[...] = st[...] * decay + update
    cd[...] = cd[...] * decay
    fin_ref[...] = st[...]
    dtot_ref[...] = cd[...]


def decay_of(cums, cums_t, head, keep):
    spread = cums[:, head : head + 1] - cums_t[head : head + 1, :]
    return jnp.where(keep, jnp.exp(jnp.where(keep, spread, 0.0)), 0.0)


def intra_kernel(hdim, heads, kq_ref, xs_ref, cums_ref, out_ref):
    ns = kq_ref.shape[1] // 2
    keys, queries = kq_ref[:, :ns], kq_ref[:, ns:]
    scores = mm(queries, keys, 1, 1)
    cums = cums_ref[...]
    cums_t = cums.T
    xs = xs_ref[...]
    keep = iota((BLOCK, BLOCK), 0) >= iota((BLOCK, BLOCK), 1)
    total = jnp.zeros(xs.shape, F32)
    for h in range(heads):
        v = (scores * decay_of(cums, cums_t, h, keep)).astype(BF16)
        total = total + mm(v, masked(xs, h, hdim))
    out_ref[...] = total


def gate_kernel(hdim, kq_ref, cums_ref, ins_ref, pre_ref, z_ref, stin_ref, cd_ref, s0_ref,
                skip_ref, gain_ref, ow_ref, c_ref, mo_ref, a_ref, y_ref, stat_ref):
    ns = kq_ref.shape[1] // 2
    ch = ins_ref.shape[1]
    hmap = head_map(ch, hdim)
    st = stin_ref[0] + cd_ref[0, 0:1, :] * s0_ref[...]
    expc = jnp.exp(mm_exact(cums_ref[...], hmap))
    carried = expc * mm(kq_ref[:, ns:], st.astype(BF16))
    px = pre_ref[...]
    xc = px * sigmoid(px)
    mo = (ins_ref[...] + carried + skip_ref[0:1, :] * xc).astype(BF16)
    mo_ref[...] = mo
    zf = z_ref[...].astype(F32)
    gated = mo.astype(F32) * (zf * sigmoid(zf))
    gain = gain_ref[0:1, :]
    y_ref[...] = mm((gated * gain).astype(BF16), ow_ref[...]).astype(BF16)
    a = mm(c_ref[...], ow_ref[...], 1, 1) * gain
    a_ref[...] = a.astype(BF16)
    sq = jnp.sum(gated * gated, axis=1, keepdims=True)
    pj = jnp.sum(gated * a, axis=1, keepdims=True)
    lanes = iota((BLOCK, LANES), 1)
    both = jnp.where(lanes == 0, sq, jnp.where(lanes == 1, pj, 0.0))
    stat_ref[...] = both.T[:8, :]


def back_gate_kernel(hdim, inner, stat_ref, mo_ref, a_ref, z_ref, c_ref, normed_ref, gain_ref, kq_ref, cums_ref,
                     do_ref, dz_ref, og_ref, gz_ref, gg_ref, dst_ref, rd_ref, g0_ref, dst, rd):
    step_id = pl.program_id(0)
    ns = kq_ref.shape[1] // 2
    ch = mo_ref.shape[1]

    @pl.when(step_id == 0)
    def _():
        dst[...] = jnp.zeros_like(dst)
        rd[...] = jnp.ones_like(rd)
        og_ref[...] = jnp.zeros_like(og_ref)
        gz_ref[...] = jnp.zeros_like(gz_ref)
        gg_ref[...] = jnp.zeros_like(gg_ref)

    stat = jnp.concatenate([stat_ref[...], jnp.zeros((LANES - 8, BLOCK), F32)], axis=0).T
    r = lax.rsqrt(stat[:, 0:1] * (1.0 / inner) + EPS)
    pj = stat[:, 1:2] * (1.0 / inner)
    mo = mo_ref[...].astype(F32)
    zf = z_ref[...].astype(F32)
    sz = sigmoid(zf)
    silu = zf * sz
    gated = mo * silu
    a = a_ref[...].astype(F32)
    n = gated * r
    gg_ref[0:1, :] += jnp.sum(a * n, axis=0, keepdims=True)
    dgated = r * (a - n * (r * pj))
    og_ref[...] += mm((n * gain_ref[0:1, :]).astype(BF16), c_ref[...], 0, 0)
    do = (dgated * silu).astype(BF16)
    do_ref[...] = do
    dz = (dgated * mo * (sz * (1.0 + zf * (1.0 - sz)))).astype(BF16)
    dz_ref[...] = dz
    gz_ref[...] += mm(normed_ref[...], dz, 0, 0)
    cums_b = mm_exact(cums_ref[...], head_map(ch, hdim))
    dst_ref[0] = dst[...]
    rd_ref[0] = rd[...]
    decay = jnp.exp(cums_b[BLOCK - 1 : BLOCK, :])
    carry = mm(kq_ref[:, ns:], (do.astype(F32) * jnp.exp(cums_b)).astype(BF16), 0, 0)
    dst[...] = dst[...] * decay + carry
    rd[...] = rd[...] * decay
    g0_ref[...] = dst[...]


def back_intra_kernel(hdim, heads, kq_ref, xs_ref, cums_ref, do_ref, dxs_ref, dkq_ref, str_ref):
    ns = kq_ref.shape[1] // 2
    keys, queries = kq_ref[:, :ns], kq_ref[:, ns:]
    scores = mm(queries, keys, 1, 1)
    cums = cums_ref[...]
    cums_t = cums.T
    xs, do = xs_ref[...], do_ref[...]
    rows, cols = iota((BLOCK, BLOCK), 0), iota((BLOCK, BLOCK), 1)
    keep = rows >= cols
    before = (rows < cols).astype(BF16)
    dxs = jnp.zeros(xs.shape, F32)
    ds = jnp.zeros((BLOCK, BLOCK), F32)
    stri = jnp.zeros((LANES, BLOCK), F32)
    lane_rows = iota((LANES, BLOCK), 0)
    for h in range(heads):
        dec = decay_of(cums, cums_t, h, keep)
        v = scores * dec
        doh = masked(do, h, hdim)
        dxs = dxs + mm(v.astype(BF16), doh, 0, 0)
        dv = mm(doh, xs, 1, 1)
        ds = ds + dv * dec
        left = mm((dv * v).astype(BF16), before)
        line = jnp.sum(jnp.where(keep, left, 0.0), axis=0, keepdims=True)
        stri = jnp.where(lane_rows == h, line, stri)
    dsl = ds.astype(BF16)
    dxs_ref[...] = dxs
    dkq_ref[:, :ns] = mm(dsl, queries, 0, 0)
    dkq_ref[:, ns:] = mm(dsl, keys)
    str_ref[...] = stri.T


def back_kernel(hdim, kq_ref, xs_ref, cums_ref, dtb_ref, pre_ref, raw_ref, do_ref, dxs_ref, dkq_ref, str_ref,
                stin_ref, cd_ref, s0_ref, dst_ref, rd_ref, inc_ref, skip_ref, cw_ref, rate_ref,
                dx_ref, ddt_ref, halo_ref, cg_ref, hg_ref, buf, rbuf):
    step_id = pl.program_id(0)
    ns = kq_ref.shape[1] // 2
    ch = xs_ref.shape[1]

    @pl.when(step_id == 0)
    def _():
        cg_ref[...] = jnp.zeros_like(cg_ref)
        hg_ref[...] = jnp.zeros_like(hg_ref)
        buf[0:PRE, :] = jnp.zeros_like(buf[0:PRE, :])
        buf[PRE + BLOCK :, :] = jnp.zeros_like(buf[PRE + BLOCK :, :])

    @pl.when(step_id > 0)
    def _():
        buf[PRE + BLOCK :, :] = buf[PRE : 2 * PRE, :]

    hmap = head_map(ch, hdim)
    keys, queries = kq_ref[:, :ns], kq_ref[:, ns:]
    cums = cums_ref[...]
    cums_b = mm_exact(cums, hmap)
    expc = jnp.exp(cums_b)
    tail = jnp.exp(cums_b[BLOCK - 1 : BLOCK, :] - cums_b)
    st = stin_ref[0] + cd_ref[0, 0:1, :] * s0_ref[...]
    dst = dst_ref[0] + rd_ref[0, 0:1, :] * inc_ref[...]
    st_low, dst_low = st.astype(BF16), dst.astype(BF16)
    do = do_ref[...].astype(F32)
    xs = xs_ref[...].astype(F32)
    carried = expc * mm(queries, st_low)
    dq = dkq_ref[:, ns:] + mm((do * expc).astype(BF16), st_low, 1, 1)
    dxs_up = tail * mm(keys, dst_low)
    dk = dkq_ref[:, :ns] + mm((xs * tail).astype(BF16), dst_low, 1, 1)
    dxs = dxs_ref[...] + dxs_up
    px = pre_ref[:, :ch]
    xc = px * sigmoid(px)
    dtb = dtb_ref[...]
    step = softplus(dtb)
    rate = rate_ref[0:1, :]
    dxc = mm_exact(step, hmap) * dxs + skip_ref[0:1, :] * do
    dstep = mm_exact(xc * dxs, hmap, 1, 1)
    arr = mm_exact(do * carried, hmap, 1, 1)
    upd = mm_exact(xs * dxs_up, hmap, 1, 1)
    rows, cols = iota((BLOCK, BLOCK), 0), iota((BLOCK, BLOCK), 1)
    through = mm_exact(jnp.sum(st * dst, axis=0, keepdims=True) * jnp.ones((8, 1), F32), hmap, 1, 1)[0:1, :]
    dlogs = (
        str_ref[...]
        + mm_exact((cols >= rows).astype(F32), arr)
        + mm_exact((cols < rows).astype(F32), upd)
        + jnp.exp(cums[BLOCK - 1 : BLOCK, :]) * through
    )
    ddtb = (dstep + dlogs * rate) * sigmoid(dtb)
    ddt_ref[...] = ddtb.astype(BF16)
    dskip = mm_exact(do * xc, hmap, 1, 1)
    hg_ref[0:1, :] += jnp.sum(ddtb, axis=0, keepdims=True)
    hg_ref[1:2, :] += jnp.sum(dlogs * step, axis=0, keepdims=True) * rate
    hg_ref[2:3, :] += jnp.sum(dskip, axis=0, keepdims=True)
    pre = pre_ref[...]
    sp = sigmoid(pre)
    dpre = jnp.concatenate([dxc, dk, dq], axis=1) * (sp * (1.0 + pre * (1.0 - sp)))
    buf[PRE : PRE + BLOCK, :] = dpre
    rbuf[...] = raw_ref[0].astype(F32)
    cg_ref[4:5, :] += jnp.sum(dpre, axis=0, keepdims=True)
    dx = jnp.zeros_like(dpre)
    halo = jnp.zeros((PRE, dpre.shape[1]), F32)
    for k in range(4):
        tap = cw_ref[k : k + 1, :]
        dx = dx + tap * buf[PRE + 3 - k : PRE + 3 - k + BLOCK, :]
        halo = halo + tap * buf[3 - k : 3 - k + PRE, :]
        cg_ref[k : k + 1, :] += jnp.sum(
            dpre * rbuf[PRE - 3 + k : PRE - 3 + k + BLOCK, :], axis=0, keepdims=True
        )
    dx_ref[...] = dx.astype(BF16)
    halo_ref[...] = halo


def rows_of(width, rows=BLOCK, rev=None):
    if rev is None:
        return pl.BlockSpec((rows, width), lambda i: (i, 0))
    return pl.BlockSpec((rows, width), lambda i: (rev - 1 - i, 0))


def slabs_of(a, b, rev=None):
    if rev is None:
        return pl.BlockSpec((1, a, b), lambda i: (i, 0, 0))
    return pl.BlockSpec((1, a, b), lambda i: (rev - 1 - i, 0, 0))


def fixed(a, b):
    return pl.BlockSpec((a, b), lambda i: (0, 0))


def sds(shape, dtype=F32):
    return jax.ShapeDtypeStruct(shape, dtype)


def shifted(values, axis, size, by):
    pairs = [(i, i + by) for i in range(size) if 0 <= i + by < size]
    return lax.ppermute(values, axis, pairs)


def gather_dp(values, axis=0):
    return lax.all_gather(values, "dp", axis=axis, tiled=True)


def carry_over(state, decay, axis, size, way):
    total = None
    for j in range(size - 1, 0, -1):
        part = shifted(state, axis, size, way * j)
        if total is None:
            total = part
        else:
            total = part + shifted(decay, axis, size, way * j)[0:1, :] * total
    return jnp.zeros_like(state) if total is None else total


def local(layer_input, norm_gain, in_weight, conv_weight, conv_bias, step_bias, rate_log, skip_gain,
          gate_gain, out_weight, cotangent):
    dp, cp, tp = lax.axis_size("dp"), lax.axis_size("cp"), lax.axis_size("tp")
    d_id, k_id = lax.axis_index("dp"), lax.axis_index("tp")
    own_rows, width = layer_input.shape
    inner = out_weight.shape[0] * dp
    conv_all = conv_weight.shape[1] * dp
    heads = step_bias.shape[0] * dp
    hdim = inner // heads
    ns = (conv_all - inner) // 2
    lh = heads // tp
    ch = inner // tp
    conv_ch = ch + 2 * ns
    tokens = own_rows * tp
    nb = tokens // BLOCK
    cols = ch + conv_ch + LANES
    taps = conv_weight.shape[0]

    x_all = lax.all_gather(layer_input, "tp", axis=0, tiled=True)
    halo = lax.all_gather(shifted(layer_input[-PRE:], "cp", cp, 1), "tp", axis=0, tiled=True)[-PRE:]
    c_all = lax.all_gather(cotangent, "tp", axis=0, tiled=True)

    def cut(values, start, size, axis=1):
        return lax.dynamic_slice_in_dim(values, start, size, axis)

    own_cols = jnp.concatenate(
        [
            cut(in_weight, k_id * ch, ch),
            cut(in_weight, inner + k_id * ch, ch),
            in_weight[:, 2 * inner : 2 * inner + 2 * ns],
            cut(in_weight, inner + conv_all + k_id * lh, lh),
            jnp.zeros((in_weight.shape[0], LANES - lh), BF16),
        ],
        axis=1,
    )
    w = gather_dp(own_cols)
    share = tp // dp
    ow = lax.all_gather(cut(out_weight, (k_id % share) * ch, ch, 0), "dp", axis=0, tiled=False)
    ow = lax.dynamic_index_in_dim(ow, k_id // share, 0, keepdims=False)
    taps_all = gather_dp(conv_weight, 1).astype(F32)
    small = gather_dp(
        jnp.concatenate([norm_gain, conv_bias, gate_gain, step_bias, rate_log, skip_gain])[None], 0
    ).astype(F32)
    widths = [width, conv_all, inner, heads, heads, heads]
    pieces, at = [], 0
    for size in widths:
        pieces.append(small[:, at : at + size // dp].reshape(-1))
        at += size // dp
    gain, offset, ggain, sbias, rlog, skip = pieces

    def own_conv(values):
        return jnp.concatenate([cut(values, k_id * ch, ch), values[:, inner:]], axis=1)

    def pad8(values):
        return jnp.pad(values, ((0, 8 - values.shape[0]), (0, 0)))

    def head_row(values):
        return jnp.pad(cut(values[None], k_id * lh, lh), ((0, 7), (0, LANES - lh)))

    cw = pad8(own_conv(taps_all))
    cb = pad8(own_conv(offset[None]))
    sb = head_row(sbias)
    rate = head_row(-jnp.exp(rlog))
    skip_b = pad8(jnp.repeat(cut(skip[None], k_id * lh, lh), hdim, axis=1))
    own_gate = pad8(cut(ggain[None], k_id * ch, ch))
    gain_row = gain[None]

    def params(**kw):
        return pltpu.CompilerParams(dimension_semantics=("arbitrary",), **kw)

    normed, z, raw, pre, xs, kq, dtb, cums, stin, cd, fin, dtot = pl.pallas_call(
        lambda *refs: front_kernel(hdim, *refs),
        grid=(nb,),
        in_specs=[rows_of(width), fixed(PRE, width), fixed(1, width), fixed(width, cols), fixed(8, conv_ch),
                  fixed(8, conv_ch), fixed(8, LANES), fixed(8, LANES)],
        out_specs=[rows_of(width), rows_of(ch), slabs_of(PRE + BLOCK, conv_ch), rows_of(conv_ch), rows_of(ch),
                   rows_of(2 * ns), rows_of(LANES), rows_of(LANES), slabs_of(ns, ch), slabs_of(8, ch),
                   fixed(ns, ch), fixed(8, ch)],
        out_shape=[sds((tokens, width), BF16), sds((tokens, ch), BF16), sds((nb, PRE + BLOCK, conv_ch), BF16),
                   sds((tokens, conv_ch)), sds((tokens, ch), BF16), sds((tokens, 2 * ns), BF16),
                   sds((tokens, LANES)), sds((tokens, LANES)), sds((nb, ns, ch)), sds((nb, 8, ch)),
                   sds((ns, ch)), sds((8, ch))],
        scratch_shapes=[pltpu.VMEM((PRE + BLOCK, conv_ch), F32), pltpu.VMEM((ns, ch), F32), pltpu.VMEM((8, ch), F32)],
        compiler_params=params(),
        name="front",
    )(x_all, halo, gain_row, w, cw, cb, sb, rate)

    s0 = carry_over(fin, dtot, "cp", cp, 1)

    inside = pl.pallas_call(
        lambda *refs: intra_kernel(hdim, lh, *refs),
        grid=(nb,),
        in_specs=[rows_of(2 * ns), rows_of(ch), rows_of(LANES)],
        out_specs=rows_of(ch),
        out_shape=sds((tokens, ch)),
        compiler_params=params(),
        name="intra",
    )(kq, xs, cums)

    mo, a, y, stat = pl.pallas_call(
        lambda *refs: gate_kernel(hdim, *refs),
        grid=(nb,),
        in_specs=[rows_of(2 * ns), rows_of(LANES), rows_of(ch), rows_of(ch), rows_of(ch), slabs_of(ns, ch),
                  slabs_of(8, ch), fixed(ns, ch), fixed(8, ch), fixed(8, ch), fixed(ch, width), rows_of(width)],
        out_specs=[rows_of(ch), rows_of(ch), rows_of(width), pl.BlockSpec((8, BLOCK), lambda i: (0, i))],
        out_shape=[sds((tokens, ch), BF16), sds((tokens, ch), BF16), sds((tokens, width), BF16), sds((8, tokens))],
        compiler_params=params(),
        name="gate",
    )(kq, cums, inside, pre, z, stin, cd, s0, skip_b, own_gate, ow, c_all)

    stats = lax.psum(stat, "tp")

    do, dz, og, gz, gg, dstl, rd, g0 = pl.pallas_call(
        lambda *refs: back_gate_kernel(hdim, inner, *refs),
        grid=(nb,),
        in_specs=[pl.BlockSpec((8, BLOCK), lambda i: (0, nb - 1 - i)), rows_of(ch, rev=nb), rows_of(ch, rev=nb),
                  rows_of(ch, rev=nb), rows_of(width, rev=nb), rows_of(width, rev=nb), fixed(8, ch),
                  rows_of(2 * ns, rev=nb), rows_of(LANES, rev=nb)],
        out_specs=[rows_of(ch, rev=nb), rows_of(ch, rev=nb), fixed(ch, width), fixed(width, ch), fixed(8, ch),
                   slabs_of(ns, ch, nb), slabs_of(8, ch, nb), fixed(ns, ch)],
        out_shape=[sds((tokens, ch), BF16), sds((tokens, ch), BF16), sds((ch, width)), sds((width, ch)), sds((8, ch)),
                   sds((nb, ns, ch)), sds((nb, 8, ch)), sds((ns, ch))],
        scratch_shapes=[pltpu.VMEM((ns, ch), F32), pltpu.VMEM((8, ch), F32)],
        compiler_params=params(),
        name="back_gate",
    )(stats, mo, a, z, c_all, normed, own_gate, kq, cums)

    incoming = carry_over(g0, dtot, "cp", cp, -1)

    dxs, dkq, stri = pl.pallas_call(
        lambda *refs: back_intra_kernel(hdim, lh, *refs),
        grid=(nb,),
        in_specs=[rows_of(2 * ns), rows_of(ch), rows_of(LANES), rows_of(ch)],
        out_specs=[rows_of(ch), rows_of(2 * ns), rows_of(LANES)],
        out_shape=[sds((tokens, ch)), sds((tokens, 2 * ns)), sds((tokens, LANES))],
        compiler_params=params(),
        name="back_intra",
    )(kq, xs, cums, do)

    dxbc, ddt, dhalo, cg, hg = pl.pallas_call(
        lambda *refs: back_kernel(hdim, *refs),
        grid=(nb,),
        in_specs=[rows_of(2 * ns, rev=nb), rows_of(ch, rev=nb), rows_of(LANES, rev=nb), rows_of(LANES, rev=nb),
                  rows_of(conv_ch, rev=nb), slabs_of(PRE + BLOCK, conv_ch, nb), rows_of(ch, rev=nb),
                  rows_of(ch, rev=nb), rows_of(2 * ns, rev=nb), rows_of(LANES, rev=nb), slabs_of(ns, ch, nb),
                  slabs_of(8, ch, nb), fixed(ns, ch), slabs_of(ns, ch, nb), slabs_of(8, ch, nb), fixed(ns, ch),
                  fixed(8, ch), fixed(8, conv_ch), fixed(8, LANES)],
        out_specs=[rows_of(conv_ch, rev=nb), rows_of(LANES, rev=nb), fixed(PRE, conv_ch), fixed(8, conv_ch),
                   fixed(8, LANES)],
        out_shape=[sds((tokens, conv_ch), BF16), sds((tokens, LANES), BF16), sds((PRE, conv_ch)), sds((8, conv_ch)),
                   sds((8, LANES))],
        scratch_shapes=[pltpu.VMEM((2 * PRE + BLOCK, conv_ch), F32), pltpu.VMEM((PRE + BLOCK, conv_ch), F32)],
        compiler_params=params(),
        name="back",
    )(kq, xs, cums, dtb, pre, raw, do, dxs, dkq, stri, stin, cd, s0, dstl, rd, incoming, skip_b, cw, rate)

    back_halo = shifted(dhalo, "cp", cp, -1)
    dxbc = jnp.concatenate([dxbc[:-PRE], (dxbc[-PRE:].astype(F32) + back_halo).astype(BF16)], axis=0)
    dproj = jnp.concatenate([dz, dxbc, ddt], axis=1)
    dn_part = mm(dproj, w, 1, 1).astype(BF16)
    grad_rest = mm(normed, dproj[:, ch:], 0, 0)

    y_own = lax.psum_scatter(y, "tp", scatter_dimension=0, tiled=True).astype(F32)
    r_own = lax.rsqrt(cut(stats, k_id * own_rows, own_rows)[0] * (1.0 / inner) + EPS)[:, None]
    u = layer_input.astype(F32)
    layer_output = (u + y_own * r_own).astype(BF16)
    dn = lax.psum_scatter(dn_part, "tp", scatter_dimension=0, tiled=True).astype(F32)
    q = lax.rsqrt(jnp.mean(u * u, axis=-1, keepdims=True) + EPS)
    m = u * q
    dg = dn * gain_row
    input_grad = cotangent.astype(F32) + q * (dg - m * jnp.mean(dg * m, axis=-1, keepdims=True))

    grp = dp * cp
    quarter = ch // grp
    src = d_id * cp + lax.axis_index("cp")
    og_low = og.astype(BF16)
    og_own = jnp.zeros((quarter, width), F32)
    for j in range(grp):
        pairs = []
        for d in range(dp):
            for p in range(cp):
                for k in range(tp):
                    piece = (d * cp + p + j) % grp
                    slot = (k % share) * grp + piece
                    pairs.append(((d * cp + p) * tp + k, (k // share) * cp * tp + slot))
        send = cut(og_low, ((src + j) % grp) * quarter, quarter, 0)
        og_own = og_own + lax.ppermute(send, ("dp", "cp", "tp"), pairs).astype(F32)
    out_grad = lax.all_gather(og_own.astype(BF16), ("cp", "tp"), axis=0, tiled=True).astype(F32)

    zx = jnp.concatenate([gz, grad_rest[:, :ch], grad_rest[:, ch + 2 * ns :]], axis=1).astype(BF16)
    zx = lax.psum_scatter(zx, "dp", scatter_dimension=0, tiled=True)
    zx = lax.psum(zx.astype(F32), "cp").astype(BF16)
    zx = lax.all_gather(zx, "tp", axis=0, tiled=False).astype(F32)
    half = zx.shape[1]
    kqg = grad_rest[:, ch : ch + 2 * ns].astype(BF16)
    kqg = lax.psum_scatter(kqg, ("dp", "cp", "tp"), scatter_dimension=0, tiled=True)
    kqg = lax.all_gather(kqg, ("cp", "tp"), axis=0, tiled=True).astype(F32)

    def across(values):
        return values.transpose(1, 0, 2).reshape(half, -1)

    in_grad = jnp.concatenate(
        [across(zx[:, :, :ch]), across(zx[:, :, ch : 2 * ch]), kqg, across(zx[:, :, 2 * ch : 2 * ch + lh])], axis=1
    )

    gain_part = jnp.sum(jnp.concatenate([gz, grad_rest], axis=1) * w.astype(F32), axis=1) / gain

    def spread(values, total, start):
        return lax.dynamic_update_slice_in_dim(
            jnp.zeros(values.shape[:-1] + (total,), F32), values, start, values.ndim - 1
        )

    def spread_conv(values):
        return jnp.concatenate([spread(values[:, :ch], inner, k_id * ch), values[:, ch:]], axis=1)

    gate_part = spread(gg[0] / own_gate[0], inner, k_id * ch)
    head_part = spread(hg[0:3, :lh], heads, k_id * lh)
    conv_part = spread_conv(cg[: taps + 1])
    gain_all, conv_sum, head_all, gate_all = lax.psum(
        (gain_part, conv_part, head_part, gate_part), ("dp", "cp", "tp")
    )

    def own(values):
        size = values.shape[-1] // dp
        return lax.dynamic_slice_in_dim(values, d_id * size, size, values.ndim - 1)

    conv_own, head_own = own(conv_sum), own(head_all)
    return (
        layer_output,
        input_grad,
        own(gain_all),
        in_grad,
        conv_own[:taps],
        conv_own[taps],
        head_own[0],
        head_own[1],
        head_own[2],
        own(gate_all),
        out_grad,
    )


def solution(mesh):
    dp, group = mesh.devices.shape
    tp = 8 if group % 8 == 0 else group
    inner_mesh = Mesh(mesh.devices.reshape(dp, group // tp, tp), ("dp", "cp", "tp"))
    tok = P(("dp", "cp", "tp"), None)
    return jax.shard_map(
        local,
        mesh=inner_mesh,
        in_specs=(tok, P("dp"), P("dp", None), P(None, "dp"), P("dp"), P("dp"), P("dp"), P("dp"), P("dp"),
                  P("dp", None), tok),
        out_specs=(tok, tok, P("dp"), P("dp", None), P(None, "dp"), P("dp"), P("dp"), P("dp"), P("dp"), P("dp"),
                   P("dp", None)),
        check_vma=False,
    )
```

```python
import jax
import jax.numpy as jnp
from jax import lax
from jax.experimental import pallas as pl
from jax.experimental.pallas import tpu as pltpu
from jax.sharding import Mesh
from jax.sharding import PartitionSpec as P

BLOCK = 256
PRE = 16
LANES = 128
EPS = 1e-05
HIGHEST = lax.Precision.HIGHEST
F32 = jnp.float32
BF16 = jnp.bfloat16


def mm(a, b, da=1, db=0):
    return lax.dot_general(a, b, (((da,), (db,)), ((), ())), preferred_element_type=F32)


def mm_exact(a, b, da=1, db=0):
    return lax.dot_general(
        a, b, (((da,), (db,)), ((), ())), precision=HIGHEST, preferred_element_type=F32
    )


def iota(shape, dim):
    return lax.broadcasted_iota(jnp.int32, shape, dim)


def head_map(channels, hdim):
    return (jnp.right_shift(iota((LANES, channels), 1), hdim.bit_length() - 1) == iota((LANES, channels), 0)).astype(F32)


def unit(u):
    return u * lax.rsqrt(jnp.mean(u * u, axis=-1, keepdims=True) + EPS)


def sigmoid(v):
    return jax.nn.sigmoid(v)


def softplus(v):
    return jnp.maximum(v, 0.0) + jnp.log1p(jnp.exp(-jnp.abs(v)))


def masked(values, head, hdim):
    lanes = iota(values.shape, 1)
    own = (lanes >= head * hdim) & (lanes < (head + 1) * hdim)
    return jnp.where(own, values, jnp.zeros_like(values))


def front_kernel(hdim, x_ref, halo_ref, gain_ref, w_ref, cw_ref, cb_ref, sb_ref, rate_ref,
                 normed_ref, z_ref, raw_ref, pre_ref, xs_ref, kq_ref, dtb_ref, cums_ref,
                 stin_ref, cd_ref, fin_ref, dtot_ref, buf, st, cd):
    step_id = pl.program_id(0)
    ch = z_ref.shape[1]
    conv_ch = pre_ref.shape[1]
    gain = gain_ref[...]

    @pl.when(step_id == 0)
    def _():
        hn = (unit(halo_ref[...].astype(F32)) * gain).astype(BF16)
        hp = mm(hn, w_ref[:, ch : ch + conv_ch])
        buf[0:PRE, :] = hp.astype(BF16).astype(F32)
        st[...] = jnp.zeros_like(st)
        cd[...] = jnp.ones_like(cd)

    @pl.when(step_id > 0)
    def _():
        buf[0:PRE, :] = buf[BLOCK : BLOCK + PRE, :]

    normed = (unit(x_ref[...].astype(F32)) * gain).astype(BF16)
    normed_ref[...] = normed
    proj = mm(normed, w_ref[...])
    z_ref[...] = proj[:, :ch].astype(BF16)
    buf[PRE : PRE + BLOCK, :] = proj[:, ch : ch + conv_ch].astype(BF16).astype(F32)
    raw_ref[0] = buf[...].astype(BF16)
    pre = cb_ref[0:1, :] + cw_ref[0:1, :] * buf[PRE - 3 : PRE - 3 + BLOCK, :]
    for k in range(1, 4):
        pre = pre + cw_ref[k : k + 1, :] * buf[PRE - 3 + k : PRE - 3 + k + BLOCK, :]
    pre_ref[...] = pre
    act = pre * sigmoid(pre)
    dtb = proj[:, ch + conv_ch :].astype(BF16).astype(F32) + sb_ref[0:1, :]
    dtb_ref[...] = dtb
    step = softplus(dtb)
    logs = step * rate_ref[0:1, :]
    lower = (iota((BLOCK, BLOCK), 0) >= iota((BLOCK, BLOCK), 1)).astype(F32)
    cums = mm_exact(lower, logs)
    cums_ref[...] = cums
    hmap = head_map(ch, hdim)
    cums_b = mm_exact(cums, hmap)
    xs = act[:, :ch] * mm_exact(step, hmap)
    xs_ref[...] = xs.astype(BF16)
    kq = act[:, ch:].astype(BF16)
    kq_ref[...] = kq
    last = cums_b[BLOCK - 1 : BLOCK, :]
    tail = jnp.exp(last - cums_b)
    update = mm(kq[:, : kq.shape[1] // 2], (xs * tail).astype(BF16), 0, 0)
    stin_ref[0] = st[...]
    cd_ref[0] = cd[...]
    decay = jnp.exp(last)
    st[...] = st[...] * decay + update
    cd[...] = cd[...] * decay
    fin_ref[...] = st[...]
    dtot_ref[...] = cd[...]


def decay_of(cums, cums_t, head, keep):
    spread = cums[:, head : head + 1] - cums_t[head : head + 1, :]
    return jnp.where(keep, jnp.exp(jnp.where(keep, spread, 0.0)), 0.0)


def intra_kernel(hdim, heads, kq_ref, xs_ref, cums_ref, out_ref):
    ns = kq_ref.shape[1] // 2
    keys, queries = kq_ref[:, :ns], kq_ref[:, ns:]
    scores = mm(queries, keys, 1, 1)
    cums = cums_ref[...]
    cums_t = cums.T
    xs = xs_ref[...]
    keep = iota((BLOCK, BLOCK), 0) >= iota((BLOCK, BLOCK), 1)
    total = jnp.zeros(xs.shape, F32)
    for h in range(heads):
        v = (scores * decay_of(cums, cums_t, h, keep)).astype(BF16)
        total = total + mm(v, masked(xs, h, hdim))
    out_ref[...] = total


def gate_kernel(hdim, kq_ref, cums_ref, ins_ref, pre_ref, z_ref, stin_ref, cd_ref, s0_ref,
                skip_ref, gain_ref, ow_ref, c_ref, mo_ref, a_ref, y_ref, stat_ref):
    ns = kq_ref.shape[1] // 2
    ch = ins_ref.shape[1]
    hmap = head_map(ch, hdim)
    st = stin_ref[0] + cd_ref[0, 0:1, :] * s0_ref[...]
    expc = jnp.exp(mm_exact(cums_ref[...], hmap))
    carried = expc * mm(kq_ref[:, ns:], st.astype(BF16))
    px = pre_ref[...]
    xc = px * sigmoid(px)
    mo = (ins_ref[...] + carried + skip_ref[0:1, :] * xc).astype(BF16)
    mo_ref[...] = mo
    zf = z_ref[...].astype(F32)
    gated = mo.astype(F32) * (zf * sigmoid(zf))
    gain = gain_ref[0:1, :]
    y_ref[...] = mm((gated * gain).astype(BF16), ow_ref[...]).astype(BF16)
    a = mm(c_ref[...], ow_ref[...], 1, 1) * gain
    a_ref[...] = a.astype(BF16)
    sq = jnp.sum(gated * gated, axis=1, keepdims=True)
    pj = jnp.sum(gated * a, axis=1, keepdims=True)
    lanes = iota((BLOCK, LANES), 1)
    both = jnp.where(lanes == 0, sq, jnp.where(lanes == 1, pj, 0.0))
    stat_ref[...] = both.T[:8, :]


def back_gate_kernel(hdim, inner, stat_ref, mo_ref, a_ref, z_ref, c_ref, normed_ref, gain_ref, kq_ref, cums_ref,
                     do_ref, dz_ref, og_ref, gz_ref, gg_ref, dst_ref, rd_ref, g0_ref, dst, rd):
    step_id = pl.program_id(0)
    ns = kq_ref.shape[1] // 2
    ch = mo_ref.shape[1]

    @pl.when(step_id == 0)
    def _():
        dst[...] = jnp.zeros_like(dst)
        rd[...] = jnp.ones_like(rd)
        og_ref[...] = jnp.zeros_like(og_ref)
        gz_ref[...] = jnp.zeros_like(gz_ref)
        gg_ref[...] = jnp.zeros_like(gg_ref)

    stat = jnp.concatenate([stat_ref[...], jnp.zeros((LANES - 8, BLOCK), F32)], axis=0).T
    r = lax.rsqrt(stat[:, 0:1] * (1.0 / inner) + EPS)
    pj = stat[:, 1:2] * (1.0 / inner)
    mo = mo_ref[...].astype(F32)
    zf = z_ref[...].astype(F32)
    sz = sigmoid(zf)
    silu = zf * sz
    gated = mo * silu
    a = a_ref[...].astype(F32)
    n = gated * r
    gg_ref[0:1, :] += jnp.sum(a * n, axis=0, keepdims=True)
    dgated = r * (a - n * (r * pj))
    og_ref[...] += mm((n * gain_ref[0:1, :]).astype(BF16), c_ref[...], 0, 0)
    do = (dgated * silu).astype(BF16)
    do_ref[...] = do
    dz = (dgated * mo * (sz * (1.0 + zf * (1.0 - sz)))).astype(BF16)
    dz_ref[...] = dz
    gz_ref[...] += mm(normed_ref[...], dz, 0, 0)
    cums_b = mm_exact(cums_ref[...], head_map(ch, hdim))
    dst_ref[0] = dst[...]
    rd_ref[0] = rd[...]
    decay = jnp.exp(cums_b[BLOCK - 1 : BLOCK, :])
    carry = mm(kq_ref[:, ns:], (do.astype(F32) * jnp.exp(cums_b)).astype(BF16), 0, 0)
    dst[...] = dst[...] * decay + carry
    rd[...] = rd[...] * decay
    g0_ref[...] = dst[...]


def back_intra_kernel(hdim, heads, kq_ref, xs_ref, cums_ref, do_ref, dxs_ref, dkq_ref, str_ref):
    ns = kq_ref.shape[1] // 2
    keys, queries = kq_ref[:, :ns], kq_ref[:, ns:]
    scores = mm(queries, keys, 1, 1)
    cums = cums_ref[...]
    cums_t = cums.T
    xs, do = xs_ref[...], do_ref[...]
    rows, cols = iota((BLOCK, BLOCK), 0), iota((BLOCK, BLOCK), 1)
    keep = rows >= cols
    before = (rows < cols).astype(BF16)
    dxs = jnp.zeros(xs.shape, F32)
    ds = jnp.zeros((BLOCK, BLOCK), F32)
    stri = jnp.zeros((LANES, BLOCK), F32)
    lane_rows = iota((LANES, BLOCK), 0)
    for h in range(heads):
        dec = decay_of(cums, cums_t, h, keep)
        v = scores * dec
        doh = masked(do, h, hdim)
        dxs = dxs + mm(v.astype(BF16), doh, 0, 0)
        dv = mm(doh, xs, 1, 1)
        ds = ds + dv * dec
        left = mm((dv * v).astype(BF16), before)
        line = jnp.sum(jnp.where(keep, left, 0.0), axis=0, keepdims=True)
        stri = jnp.where(lane_rows == h, line, stri)
    dsl = ds.astype(BF16)
    dxs_ref[...] = dxs
    dkq_ref[:, :ns] = mm(dsl, queries, 0, 0)
    dkq_ref[:, ns:] = mm(dsl, keys)
    str_ref[...] = stri.T


def back_kernel(hdim, kq_ref, xs_ref, cums_ref, dtb_ref, pre_ref, raw_ref, do_ref, dxs_ref, dkq_ref, str_ref,
                stin_ref, cd_ref, s0_ref, dst_ref, rd_ref, inc_ref, skip_ref, cw_ref, rate_ref,
                dx_ref, ddt_ref, halo_ref, cg_ref, hg_ref, buf, rbuf):
    step_id = pl.program_id(0)
    ns = kq_ref.shape[1] // 2
    ch = xs_ref.shape[1]

    @pl.when(step_id == 0)
    def _():
        cg_ref[...] = jnp.zeros_like(cg_ref)
        hg_ref[...] = jnp.zeros_like(hg_ref)
        buf[0:PRE, :] = jnp.zeros_like(buf[0:PRE, :])
        buf[PRE + BLOCK :, :] = jnp.zeros_like(buf[PRE + BLOCK :, :])

    @pl.when(step_id > 0)
    def _():
        buf[PRE + BLOCK :, :] = buf[PRE : 2 * PRE, :]

    hmap = head_map(ch, hdim)
    keys, queries = kq_ref[:, :ns], kq_ref[:, ns:]
    cums = cums_ref[...]
    cums_b = mm_exact(cums, hmap)
    expc = jnp.exp(cums_b)
    tail = jnp.exp(cums_b[BLOCK - 1 : BLOCK, :] - cums_b)
    st = stin_ref[0] + cd_ref[0, 0:1, :] * s0_ref[...]
    dst = dst_ref[0] + rd_ref[0, 0:1, :] * inc_ref[...]
    st_low, dst_low = st.astype(BF16), dst.astype(BF16)
    do = do_ref[...].astype(F32)
    xs = xs_ref[...].astype(F32)
    carried = expc * mm(queries, st_low)
    dq = dkq_ref[:, ns:] + mm((do * expc).astype(BF16), st_low, 1, 1)
    dxs_up = tail * mm(keys, dst_low)
    dk = dkq_ref[:, :ns] + mm((xs * tail).astype(BF16), dst_low, 1, 1)
    dxs = dxs_ref[...] + dxs_up
    px = pre_ref[:, :ch]
    xc = px * sigmoid(px)
    dtb = dtb_ref[...]
    step = softplus(dtb)
    rate = rate_ref[0:1, :]
    dxc = mm_exact(step, hmap) * dxs + skip_ref[0:1, :] * do
    dstep = mm_exact(xc * dxs, hmap, 1, 1)
    arr = mm_exact(do * carried, hmap, 1, 1)
    upd = mm_exact(xs * dxs_up, hmap, 1, 1)
    rows, cols = iota((BLOCK, BLOCK), 0), iota((BLOCK, BLOCK), 1)
    through = mm_exact(jnp.sum(st * dst, axis=0, keepdims=True) * jnp.ones((8, 1), F32), hmap, 1, 1)[0:1, :]
    dlogs = (
        str_ref[...]
        + mm_exact((cols >= rows).astype(F32), arr)
        + mm_exact((cols < rows).astype(F32), upd)
        + jnp.exp(cums[BLOCK - 1 : BLOCK, :]) * through
    )
    ddtb = (dstep + dlogs * rate) * sigmoid(dtb)
    ddt_ref[...] = ddtb.astype(BF16)
    dskip = mm_exact(do * xc, hmap, 1, 1)
    hg_ref[0:1, :] += jnp.sum(ddtb, axis=0, keepdims=True)
    hg_ref[1:2, :] += jnp.sum(dlogs * step, axis=0, keepdims=True) * rate
    hg_ref[2:3, :] += jnp.sum(dskip, axis=0, keepdims=True)
    pre = pre_ref[...]
    sp = sigmoid(pre)
    dpre = jnp.concatenate([dxc, dk, dq], axis=1) * (sp * (1.0 + pre * (1.0 - sp)))
    buf[PRE : PRE + BLOCK, :] = dpre
    rbuf[...] = raw_ref[0].astype(F32)
    cg_ref[4:5, :] += jnp.sum(dpre, axis=0, keepdims=True)
    dx = jnp.zeros_like(dpre)
    halo = jnp.zeros((PRE, dpre.shape[1]), F32)
    for k in range(4):
        tap = cw_ref[k : k + 1, :]
        dx = dx + tap * buf[PRE + 3 - k : PRE + 3 - k + BLOCK, :]
        halo = halo + tap * buf[3 - k : 3 - k + PRE, :]
        cg_ref[k : k + 1, :] += jnp.sum(
            dpre * rbuf[PRE - 3 + k : PRE - 3 + k + BLOCK, :], axis=0, keepdims=True
        )
    dx_ref[...] = dx.astype(BF16)
    halo_ref[...] = halo


def assemble_kernel(ch, inner, z_ref, x_ref, kq_ref, out_ref):
    for k in range(z_ref.shape[0]):
        out_ref[:, k * ch : (k + 1) * ch] = z_ref[k].astype(F32)
        out_ref[:, inner + k * ch : inner + (k + 1) * ch] = x_ref[k].astype(F32)
    out_ref[:, 2 * inner :] = kq_ref[:, : out_ref.shape[1] - 2 * inner].astype(F32)


def rows_of(width, rows=BLOCK, rev=None):
    if rev is None:
        return pl.BlockSpec((rows, width), lambda i: (i, 0))
    return pl.BlockSpec((rows, width), lambda i: (rev - 1 - i, 0))


def slabs_of(a, b, rev=None):
    if rev is None:
        return pl.BlockSpec((1, a, b), lambda i: (i, 0, 0))
    return pl.BlockSpec((1, a, b), lambda i: (rev - 1 - i, 0, 0))


def fixed(a, b):
    return pl.BlockSpec((a, b), lambda i: (0, 0))


def sds(shape, dtype=F32):
    return jax.ShapeDtypeStruct(shape, dtype)


def shifted(values, axis, size, by):
    pairs = [(i, i + by) for i in range(size) if 0 <= i + by < size]
    return lax.ppermute(values, axis, pairs)


def gather_dp(values, dp, d_id):
    parts = [values] + [
        lax.ppermute(values, "dp", [(i, (i - j) % dp) for i in range(dp)]) for j in range(1, dp)
    ]
    if dp == 2:
        first = d_id == 0
        return jnp.stack([jnp.where(first, parts[0], parts[1]), jnp.where(first, parts[1], parts[0])])
    stacked = jnp.stack(parts)
    return jnp.take(stacked, (jnp.arange(dp) - d_id) % dp, axis=0)


def scatter_dp(values, dp, d_id, axis=0):
    size = values.shape[axis] // dp

    def part(index):
        return lax.dynamic_slice_in_dim(values, index * size, size, axis)

    total = part(d_id)
    for j in range(1, dp):
        sent = part((d_id + j) % dp).astype(BF16)
        total = total + lax.ppermute(sent, "dp", [(i, (i + j) % dp) for i in range(dp)]).astype(F32)
    return total


def swap(values, axis, size, bit):
    return lax.ppermute(values, axis, [(i, i ^ bit) for i in range(size)])


def sum_over(values, axis, size, kind=F32):
    bit = 1
    while bit < size:
        values = values + swap(values.astype(kind), axis, size, bit).astype(F32)
        bit *= 2
    return values


def scatter_over(values, axis, size, index):
    bit = size // 2
    while bit:
        half = values.shape[0] // 2
        upper = (index & bit) != 0
        low, high = values[:half], values[half:]
        kept = jnp.where(upper, high, low)
        sent = jnp.where(upper, low, high).astype(BF16)
        values = kept + swap(sent, axis, size, bit).astype(F32)
        bit //= 2
    return values


def gather_over(values, axis, size, index):
    bit = 1
    while bit < size:
        other = swap(values, axis, size, bit)
        upper = (index & bit) != 0
        values = jnp.concatenate([jnp.where(upper, other, values), jnp.where(upper, values, other)], axis=0)
        bit *= 2
    return values


def carry_over(state, decay, axis, size, way):
    total = None
    for j in range(size - 1, 0, -1):
        part = shifted(state, axis, size, way * j)
        if total is None:
            total = part
        else:
            total = part + shifted(decay, axis, size, way * j)[0:1, :] * total
    return jnp.zeros_like(state) if total is None else total


def local(layer_input, norm_gain, in_weight, conv_weight, conv_bias, step_bias, rate_log, skip_gain,
          gate_gain, out_weight, cotangent):
    dp, cp, tp = lax.axis_size("dp"), lax.axis_size("cp"), lax.axis_size("tp")
    d_id, k_id = lax.axis_index("dp"), lax.axis_index("tp")
    own_rows, width = layer_input.shape
    inner = out_weight.shape[0] * dp
    conv_all = conv_weight.shape[1] * dp
    heads = step_bias.shape[0] * dp
    hdim = inner // heads
    ns = (conv_all - inner) // 2
    lh = heads // tp
    ch = inner // tp
    conv_ch = ch + 2 * ns
    tokens = own_rows * tp
    nb = tokens // BLOCK
    cols = ch + conv_ch + LANES
    taps = conv_weight.shape[0]

    def cut(values, start, size, axis=1):
        return lax.dynamic_slice_in_dim(values, start, size, axis)

    share = tp // dp
    own_cols = jnp.concatenate(
        [
            cut(in_weight, k_id * ch, ch),
            cut(in_weight, inner + k_id * ch, ch),
            in_weight[:, 2 * inner : 2 * inner + 2 * ns],
            cut(in_weight, inner + conv_all + k_id * lh, lh),
            jnp.zeros((in_weight.shape[0], LANES - lh), BF16),
        ],
        axis=1,
    )
    row_size = conv_all // dp

    def wide(values):
        return jnp.pad(values, ((0, 0), (0, row_size - values.shape[1])))

    heads_own = jnp.concatenate([step_bias, rate_log, skip_gain])[None]
    small = jnp.concatenate(
        [conv_weight, conv_bias[None], wide(norm_gain[None]), wide(gate_gain[None]), wide(heads_own)], axis=0
    )
    small = gather_dp(small, dp, d_id).astype(F32)
    w = gather_dp(own_cols, dp, d_id).reshape(width, cols)
    x_all = lax.all_gather(layer_input, "tp", axis=0, tiled=True)
    halo = lax.all_gather(shifted(layer_input[-PRE:], "cp", cp, 1), "tp", axis=0, tiled=True)[-PRE:]
    c_all = lax.all_gather(cotangent, "tp", axis=0, tiled=True)
    ow = gather_dp(cut(out_weight, (k_id % share) * ch, ch, 0), dp, d_id)
    ow = lax.dynamic_index_in_dim(ow, k_id // share, 0, keepdims=False)

    def row_of(index, size, at=0):
        return small[:, index, at : at + size].reshape(-1)

    taps_all = small[:, :taps].transpose(1, 0, 2).reshape(taps, conv_all)
    offset = row_of(taps, row_size)
    gain = row_of(taps + 1, width // dp)
    ggain = row_of(taps + 2, inner // dp)
    hs = heads // dp
    sbias, rlog, skip = (row_of(taps + 3, hs, i * hs) for i in range(3))

    def own_conv(values):
        return jnp.concatenate([cut(values, k_id * ch, ch), values[:, inner:]], axis=1)

    def pad8(values):
        return jnp.pad(values, ((0, 8 - values.shape[0]), (0, 0)))

    def head_row(values):
        return jnp.pad(cut(values[None], k_id * lh, lh), ((0, 7), (0, LANES - lh)))

    cw = pad8(own_conv(taps_all))
    cb = pad8(own_conv(offset[None]))
    sb = head_row(sbias)
    rate = head_row(-jnp.exp(rlog))
    skip_b = pad8(jnp.repeat(cut(skip[None], k_id * lh, lh), hdim, axis=1))
    own_gate = pad8(cut(ggain[None], k_id * ch, ch))
    gain_row = gain[None]

    def params(**kw):
        return pltpu.CompilerParams(dimension_semantics=("arbitrary",), **kw)

    normed, z, raw, pre, xs, kq, dtb, cums, stin, cd, fin, dtot = pl.pallas_call(
        lambda *refs: front_kernel(hdim, *refs),
        grid=(nb,),
        in_specs=[rows_of(width), fixed(PRE, width), fixed(1, width), fixed(width, cols), fixed(8, conv_ch),
                  fixed(8, conv_ch), fixed(8, LANES), fixed(8, LANES)],
        out_specs=[rows_of(width), rows_of(ch), slabs_of(PRE + BLOCK, conv_ch), rows_of(conv_ch), rows_of(ch),
                   rows_of(2 * ns), rows_of(LANES), rows_of(LANES), slabs_of(ns, ch), slabs_of(8, ch),
                   fixed(ns, ch), fixed(8, ch)],
        out_shape=[sds((tokens, width), BF16), sds((tokens, ch), BF16), sds((nb, PRE + BLOCK, conv_ch), BF16),
                   sds((tokens, conv_ch)), sds((tokens, ch), BF16), sds((tokens, 2 * ns), BF16),
                   sds((tokens, LANES)), sds((tokens, LANES)), sds((nb, ns, ch)), sds((nb, 8, ch)),
                   sds((ns, ch)), sds((8, ch))],
        scratch_shapes=[pltpu.VMEM((PRE + BLOCK, conv_ch), F32), pltpu.VMEM((ns, ch), F32), pltpu.VMEM((8, ch), F32)],
        compiler_params=params(),
        name="front",
    )(x_all, halo, gain_row, w, cw, cb, sb, rate)

    s0 = carry_over(fin, dtot, "cp", cp, 1)

    inside = pl.pallas_call(
        lambda *refs: intra_kernel(hdim, lh, *refs),
        grid=(nb,),
        in_specs=[rows_of(2 * ns), rows_of(ch), rows_of(LANES)],
        out_specs=rows_of(ch),
        out_shape=sds((tokens, ch)),
        compiler_params=params(),
        name="intra",
    )(kq, xs, cums)

    mo, a, y, stat = pl.pallas_call(
        lambda *refs: gate_kernel(hdim, *refs),
        grid=(nb,),
        in_specs=[rows_of(2 * ns), rows_of(LANES), rows_of(ch), rows_of(ch), rows_of(ch), slabs_of(ns, ch),
                  slabs_of(8, ch), fixed(ns, ch), fixed(8, ch), fixed(8, ch), fixed(ch, width), rows_of(width)],
        out_specs=[rows_of(ch), rows_of(ch), rows_of(width), pl.BlockSpec((8, BLOCK), lambda i: (0, i))],
        out_shape=[sds((tokens, ch), BF16), sds((tokens, ch), BF16), sds((tokens, width), BF16), sds((8, tokens))],
        compiler_params=params(),
        name="gate",
    )(kq, cums, inside, pre, z, stin, cd, s0, skip_b, own_gate, ow, c_all)

    stats = sum_over(stat, "tp", tp)

    do, dz, og, gz, gg, dstl, rd, g0 = pl.pallas_call(
        lambda *refs: back_gate_kernel(hdim, inner, *refs),
        grid=(nb,),
        in_specs=[pl.BlockSpec((8, BLOCK), lambda i: (0, nb - 1 - i)), rows_of(ch, rev=nb), rows_of(ch, rev=nb),
                  rows_of(ch, rev=nb), rows_of(width, rev=nb), rows_of(width, rev=nb), fixed(8, ch),
                  rows_of(2 * ns, rev=nb), rows_of(LANES, rev=nb)],
        out_specs=[rows_of(ch, rev=nb), rows_of(ch, rev=nb), fixed(ch, width), fixed(width, ch), fixed(8, ch),
                   slabs_of(ns, ch, nb), slabs_of(8, ch, nb), fixed(ns, ch)],
        out_shape=[sds((tokens, ch), BF16), sds((tokens, ch), BF16), sds((ch, width)), sds((width, ch)), sds((8, ch)),
                   sds((nb, ns, ch)), sds((nb, 8, ch)), sds((ns, ch))],
        scratch_shapes=[pltpu.VMEM((ns, ch), F32), pltpu.VMEM((8, ch), F32)],
        compiler_params=params(),
        name="back_gate",
    )(stats, mo, a, z, c_all, normed, own_gate, kq, cums)

    incoming = carry_over(g0, dtot, "cp", cp, -1)

    dxs, dkq, stri = pl.pallas_call(
        lambda *refs: back_intra_kernel(hdim, lh, *refs),
        grid=(nb,),
        in_specs=[rows_of(2 * ns), rows_of(ch), rows_of(LANES), rows_of(ch)],
        out_specs=[rows_of(ch), rows_of(2 * ns), rows_of(LANES)],
        out_shape=[sds((tokens, ch)), sds((tokens, 2 * ns)), sds((tokens, LANES))],
        compiler_params=params(),
        name="back_intra",
    )(kq, xs, cums, do)

    dxbc, ddt, dhalo, cg, hg = pl.pallas_call(
        lambda *refs: back_kernel(hdim, *refs),
        grid=(nb,),
        in_specs=[rows_of(2 * ns, rev=nb), rows_of(ch, rev=nb), rows_of(LANES, rev=nb), rows_of(LANES, rev=nb),
                  rows_of(conv_ch, rev=nb), slabs_of(PRE + BLOCK, conv_ch, nb), rows_of(ch, rev=nb),
                  rows_of(ch, rev=nb), rows_of(2 * ns, rev=nb), rows_of(LANES, rev=nb), slabs_of(ns, ch, nb),
                  slabs_of(8, ch, nb), fixed(ns, ch), slabs_of(ns, ch, nb), slabs_of(8, ch, nb), fixed(ns, ch),
                  fixed(8, ch), fixed(8, conv_ch), fixed(8, LANES)],
        out_specs=[rows_of(conv_ch, rev=nb), rows_of(LANES, rev=nb), fixed(PRE, conv_ch), fixed(8, conv_ch),
                   fixed(8, LANES)],
        out_shape=[sds((tokens, conv_ch), BF16), sds((tokens, LANES), BF16), sds((PRE, conv_ch)), sds((8, conv_ch)),
                   sds((8, LANES))],
        scratch_shapes=[pltpu.VMEM((2 * PRE + BLOCK, conv_ch), F32), pltpu.VMEM((PRE + BLOCK, conv_ch), F32)],
        compiler_params=params(),
        name="back",
    )(kq, xs, cums, dtb, pre, raw, do, dxs, dkq, stri, stin, cd, s0, dstl, rd, incoming, skip_b, cw, rate)

    back_halo = shifted(dhalo, "cp", cp, -1)
    dxbc = jnp.concatenate([dxbc[:-PRE], (dxbc[-PRE:].astype(F32) + back_halo).astype(BF16)], axis=0)
    dproj = jnp.concatenate([dz, dxbc, ddt], axis=1)
    dn_part = mm(dproj, w, 1, 1).astype(BF16)
    grad_rest = mm(normed, dproj[:, ch:], 0, 0)

    y_own = lax.psum_scatter(y, "tp", scatter_dimension=0, tiled=True).astype(F32)
    r_own = lax.rsqrt(cut(stats, k_id * own_rows, own_rows)[0] * (1.0 / inner) + EPS)[:, None]
    u = layer_input.astype(F32)
    layer_output = (u + y_own * r_own).astype(BF16)
    dn = lax.psum_scatter(dn_part, "tp", scatter_dimension=0, tiled=True).astype(F32)
    q = lax.rsqrt(jnp.mean(u * u, axis=-1, keepdims=True) + EPS)
    m = u * q
    dg = dn * gain_row
    input_grad = cotangent.astype(F32) + q * (dg - m * jnp.mean(dg * m, axis=-1, keepdims=True))

    grp = dp * cp
    quarter = ch // grp
    c_id = lax.axis_index("cp")
    src = d_id * cp + c_id
    og_low = og.astype(BF16)
    og_own = jnp.zeros((quarter, width), F32)
    for j in range(grp):
        pairs = []
        for d in range(dp):
            for p in range(cp):
                for k in range(tp):
                    piece = (d * cp + p + j) % grp
                    slot = (k % share) * grp + piece
                    pairs.append(((d * cp + p) * tp + k, (k // share) * cp * tp + (slot % cp) * tp + slot // cp))
        send = cut(og_low, ((src + j) % grp) * quarter, quarter, 0)
        og_own = og_own + lax.ppermute(send, ("dp", "cp", "tp"), pairs).astype(F32)
    og_own = gather_over(og_own.astype(BF16), "cp", cp, c_id)
    out_grad = lax.all_gather(og_own, "tp", axis=0, tiled=True).astype(F32)

    def total_of(values):
        return sum_over(scatter_dp(values, dp, d_id), "cp", cp, BF16)

    zg = lax.all_gather(total_of(gz).astype(BF16), "tp", axis=0, tiled=False)
    xg = lax.all_gather(total_of(grad_rest[:, :ch]).astype(BF16), "tp", axis=0, tiled=False)
    dt_grad = lax.dynamic_update_slice_in_dim(
        jnp.zeros((width, LANES), F32), grad_rest[:, ch + 2 * ns : ch + 2 * ns + lh], k_id * lh, 1
    )
    kqg = total_of(jnp.concatenate([grad_rest[:, ch : ch + 2 * ns], dt_grad], axis=1))
    kqg = scatter_over(kqg, "tp", tp, k_id).astype(BF16)
    kqg = gather_over(kqg, "tp", tp, k_id)
    half = kqg.shape[0]
    tile = 64
    proj_all = in_weight.shape[1]
    in_grad = pl.pallas_call(
        lambda *refs: assemble_kernel(ch, inner, *refs),
        grid=(half // tile,),
        in_specs=[pl.BlockSpec((tp, tile, ch), lambda i: (0, i, 0)), pl.BlockSpec((tp, tile, ch), lambda i: (0, i, 0)),
                  rows_of(2 * ns + LANES, tile)],
        out_specs=rows_of(proj_all, tile),
        out_shape=sds((half, proj_all)),
        compiler_params=params(),
        name="assemble",
    )(zg, xg, kqg)

    gain_part = jnp.sum(jnp.concatenate([gz, grad_rest], axis=1) * w.astype(F32), axis=1) / gain

    def spread(values, total, start):
        return lax.dynamic_update_slice_in_dim(
            jnp.zeros(values.shape[:-1] + (total,), F32), values, start, values.ndim - 1
        )

    def spread_conv(values):
        return jnp.concatenate([spread(values[:, :ch], inner, k_id * ch), values[:, ch:]], axis=1)

    def full(values):
        return jnp.pad(values, ((0, 0), (0, conv_all - values.shape[1])))

    conv_part = spread_conv(cg[: taps + 1])
    gate_part = spread(gg[0:1] / own_gate[0:1], inner, k_id * ch)
    head_part = spread(hg[0:3, :lh], heads, k_id * lh).reshape(1, 3 * heads)
    pack = jnp.concatenate([conv_part, full(gate_part), full(gain_part[None]), full(head_part)], axis=0)
    pack = sum_over(sum_over(sum_over(pack, "tp", tp), "cp", cp), "dp", dp)

    def own(values):
        size = values.shape[-1] // dp
        return lax.dynamic_slice_in_dim(values, d_id * size, size, values.ndim - 1)

    conv_own = own(pack[: taps + 1])
    head_own = own(pack[taps + 3, : 3 * heads].reshape(3, heads))
    gate_all, gain_all = pack[taps + 1, :inner], pack[taps + 2, :width]
    return (
        layer_output,
        input_grad,
        own(gain_all),
        in_grad,
        conv_own[:taps],
        conv_own[taps],
        head_own[0],
        head_own[1],
        head_own[2],
        own(gate_all),
        out_grad,
    )


def solution(mesh):
    dp, group = mesh.devices.shape
    tp = 8 if group % 8 == 0 else group
    inner_mesh = Mesh(mesh.devices.reshape(dp, group // tp, tp), ("dp", "cp", "tp"))
    tok = P(("dp", "cp", "tp"), None)
    return jax.shard_map(
        local,
        mesh=inner_mesh,
        in_specs=(tok, P("dp"), P("dp", None), P(None, "dp"), P("dp"), P("dp"), P("dp"), P("dp"), P("dp"),
                  P("dp", None), tok),
        out_specs=(tok, tok, P("dp"), P("dp", None), P(None, "dp"), P("dp"), P("dp"), P("dp"), P("dp"), P("dp"),
                   P("dp", None)),
        check_vma=False,
    )
```

```python
import jax
import jax.numpy as jnp
from jax import lax
from jax.experimental import pallas as pl
from jax.experimental.pallas import tpu as pltpu
from jax.sharding import Mesh
from jax.sharding import PartitionSpec as P

BLOCK = 256
PRE = 16
LANES = 128
EPS = 1e-05
F32 = jnp.float32
BF16 = jnp.bfloat16


def mm(a, b, da=1, db=0):
    return lax.dot_general(a, b, (((da,), (db,)), ((), ())), preferred_element_type=F32)


def mm_parts(a, b, parts, da=1, db=0):
    total = None
    for _ in range(parts):
        high = a.astype(BF16)
        term = mm(high, b, da, db)
        total = term if total is None else total + term
        a = a - high.astype(F32)
    return total


def iota(shape, dim):
    return lax.broadcasted_iota(jnp.int32, shape, dim)


def head_map(channels, hdim):
    return (jnp.right_shift(iota((LANES, channels), 1), hdim.bit_length() - 1) == iota((LANES, channels), 0)).astype(BF16)


def unit(u):
    return u * lax.rsqrt(jnp.mean(u * u, axis=-1, keepdims=True) + EPS)


def sigmoid(v):
    return jax.nn.sigmoid(v)


def softplus(v):
    return jnp.maximum(v, 0.0) + jnp.log1p(jnp.exp(-jnp.abs(v)))


def masked(values, head, hdim):
    lanes = iota(values.shape, 1)
    own = (lanes >= head * hdim) & (lanes < (head + 1) * hdim)
    return jnp.where(own, values, jnp.zeros_like(values))


def front_kernel(hdim, x_ref, halo_ref, gain_ref, w_ref, cw_ref, cb_ref, sb_ref, rate_ref,
                 normed_ref, z_ref, raw_ref, pre_ref, xs_ref, kq_ref, dtb_ref, cums_ref, expc_ref, tail_ref, stepb_ref,
                 stin_ref, cd_ref, fin_ref, dtot_ref, buf, st, cd):
    step_id = pl.program_id(0)
    ch = z_ref.shape[1]
    conv_ch = pre_ref.shape[1]
    gain = gain_ref[...]

    @pl.when(step_id == 0)
    def _():
        hn = (unit(halo_ref[...].astype(F32)) * gain).astype(BF16)
        hp = mm(hn, w_ref[ch : ch + conv_ch, :], 1, 1)
        buf[0:PRE, :] = hp.astype(BF16).astype(F32)
        st[...] = jnp.zeros_like(st)
        cd[...] = jnp.ones_like(cd)

    @pl.when(step_id > 0)
    def _():
        buf[0:PRE, :] = buf[BLOCK : BLOCK + PRE, :]

    normed = (unit(x_ref[...].astype(F32)) * gain).astype(BF16)
    normed_ref[...] = normed
    proj = mm(normed, w_ref[...], 1, 1)
    z_ref[...] = proj[:, :ch].astype(BF16)
    buf[PRE : PRE + BLOCK, :] = proj[:, ch : ch + conv_ch].astype(BF16).astype(F32)
    raw_ref[0] = buf[...].astype(BF16)
    pre = cb_ref[0:1, :] + cw_ref[0:1, :] * buf[PRE - 3 : PRE - 3 + BLOCK, :]
    for k in range(1, 4):
        pre = pre + cw_ref[k : k + 1, :] * buf[PRE - 3 + k : PRE - 3 + k + BLOCK, :]
    pre_ref[...] = pre
    act = pre * sigmoid(pre)
    dtb = proj[:, ch + conv_ch :].astype(BF16).astype(F32) + sb_ref[0:1, :]
    dtb_ref[...] = dtb
    step = softplus(dtb)
    logs = step * rate_ref[0:1, :]
    upper = (iota((BLOCK, BLOCK), 0) <= iota((BLOCK, BLOCK), 1)).astype(BF16)
    cums = mm_parts(logs.T[:8, :], upper, 3)
    cums = jnp.concatenate([cums, jnp.zeros((LANES - 8, BLOCK), F32)], axis=0).T
    cums_ref[...] = cums
    hmap = head_map(ch, hdim)
    cums_b = mm_parts(cums, hmap, 3)
    step_b = mm_parts(step, hmap, 2)
    stepb_ref[...] = step_b.astype(BF16)
    xs = act[:, :ch] * step_b
    xs_ref[...] = xs.astype(BF16)
    kq = act[:, ch:].astype(BF16)
    kq_ref[...] = kq
    last = cums_b[BLOCK - 1 : BLOCK, :]
    tail = jnp.exp(last - cums_b)
    tail_ref[...] = tail.astype(BF16)
    expc_ref[...] = jnp.exp(cums_b).astype(BF16)
    update = mm(kq[:, : kq.shape[1] // 2], (xs * tail).astype(BF16), 0, 0)
    stin_ref[0] = st[...]
    cd_ref[0] = cd[...]
    decay = jnp.exp(last)
    st[...] = st[...] * decay + update
    cd[...] = cd[...] * decay
    fin_ref[...] = st[...]
    dtot_ref[...] = cd[...]


def decay_of(cums, cums_t, head, keep):
    spread = cums[:, head : head + 1] - cums_t[head : head + 1, :]
    return jnp.where(keep, jnp.exp(jnp.where(keep, spread, 0.0)), 0.0)


def intra_kernel(hdim, heads, kq_ref, xs_ref, cums_ref, out_ref):
    ns = kq_ref.shape[1] // 2
    keys, queries = kq_ref[:, :ns], kq_ref[:, ns:]
    scores = mm(queries, keys, 1, 1)
    cums = cums_ref[...]
    cums_t = cums.T
    xs = xs_ref[...]
    keep = iota((BLOCK, BLOCK), 0) >= iota((BLOCK, BLOCK), 1)
    total = jnp.zeros(xs.shape, F32)
    for h in range(heads):
        v = (scores * decay_of(cums, cums_t, h, keep)).astype(BF16)
        total = total + mm(v, masked(xs, h, hdim))
    out_ref[...] = total


def gate_kernel(kq_ref, expc_ref, ins_ref, pre_ref, z_ref, stin_ref, cd_ref, s0_ref,
                skip_ref, gain_ref, ow_ref, c_ref, mo_ref, a_ref, y_ref, stat_ref):
    ns = kq_ref.shape[1] // 2
    ch = ins_ref.shape[1]
    st = stin_ref[0] + cd_ref[0, 0:1, :] * s0_ref[...]
    carried = expc_ref[...].astype(F32) * mm(kq_ref[:, ns:], st.astype(BF16))
    px = pre_ref[...]
    xc = px * sigmoid(px)
    mo = (ins_ref[...] + carried + skip_ref[0:1, :] * xc).astype(BF16)
    mo_ref[...] = mo
    zf = z_ref[...].astype(F32)
    gated = mo.astype(F32) * (zf * sigmoid(zf))
    gain = gain_ref[0:1, :]
    y_ref[...] = mm((gated * gain).astype(BF16), ow_ref[...]).astype(BF16)
    a = mm(c_ref[...], ow_ref[...], 1, 1) * gain
    a_ref[...] = a.astype(BF16)
    sq = jnp.sum(gated * gated, axis=1, keepdims=True)
    pj = jnp.sum(gated * a, axis=1, keepdims=True)
    lanes = iota((BLOCK, LANES), 1)
    both = jnp.where(lanes == 0, sq, jnp.where(lanes == 1, pj, 0.0))
    stat_ref[...] = both.T[:8, :]


def back_gate_kernel(inner, stat_ref, mo_ref, a_ref, z_ref, c_ref, normed_ref, gain_ref, kq_ref, expc_ref, w_ref,
                     do_ref, dz_ref, og_ref, gz_ref, gg_ref, gs_ref, dst_ref, rd_ref, g0_ref, dst, rd, og, gz):
    step_id = pl.program_id(0)
    ns = kq_ref.shape[1] // 2

    @pl.when(step_id == 0)
    def _():
        dst[...] = jnp.zeros_like(dst)
        rd[...] = jnp.ones_like(rd)
        og[...] = jnp.zeros_like(og)
        gz[...] = jnp.zeros_like(gz)
        gg_ref[...] = jnp.zeros_like(gg_ref)

    stat = jnp.concatenate([stat_ref[...], jnp.zeros((LANES - 8, BLOCK), F32)], axis=0).T
    r = lax.rsqrt(stat[:, 0:1] * (1.0 / inner) + EPS)
    pj = stat[:, 1:2] * (1.0 / inner)
    mo = mo_ref[...].astype(F32)
    zf = z_ref[...].astype(F32)
    sz = sigmoid(zf)
    silu = zf * sz
    gated = mo * silu
    a = a_ref[...].astype(F32)
    n = gated * r
    gg_ref[0:1, :] += jnp.sum(a * n, axis=0, keepdims=True)
    dgated = r * (a - n * (r * pj))
    og[...] += mm((n * gain_ref[0:1, :]).astype(BF16), c_ref[...], 0, 0)
    do = (dgated * silu).astype(BF16)
    do_ref[...] = do
    dz = (dgated * mo * (sz * (1.0 + zf * (1.0 - sz)))).astype(BF16)
    dz_ref[...] = dz
    gz[...] += mm(dz, normed_ref[...], 0, 0)
    expc = expc_ref[...].astype(F32)
    dst_ref[0] = dst[...]
    rd_ref[0] = rd[...]
    decay = expc[BLOCK - 1 : BLOCK, :]
    carry = mm(kq_ref[:, ns:], (do.astype(F32) * expc).astype(BF16), 0, 0)
    dst[...] = dst[...] * decay + carry
    rd[...] = rd[...] * decay
    g0_ref[...] = dst[...]

    @pl.when(step_id == pl.num_programs(0) - 1)
    def _():
        og_ref[...] = og[...].astype(BF16)
        gz_ref[...] = gz[...].astype(BF16)
        gs_ref[...] = jnp.broadcast_to(
            jnp.sum(gz[...] * w_ref[...].astype(F32), axis=0, keepdims=True), gs_ref.shape
        )


def back_intra_kernel(hdim, heads, kq_ref, xs_ref, cums_ref, do_ref, dxs_ref, dkq_ref, str_ref):
    ns = kq_ref.shape[1] // 2
    keys, queries = kq_ref[:, :ns], kq_ref[:, ns:]
    scores = mm(queries, keys, 1, 1)
    cums = cums_ref[...]
    cums_t = cums.T
    xs, do = xs_ref[...], do_ref[...]
    rows, cols = iota((BLOCK, BLOCK), 0), iota((BLOCK, BLOCK), 1)
    keep = rows >= cols
    before = (rows < cols).astype(BF16)
    dxs = jnp.zeros(xs.shape, F32)
    ds = jnp.zeros((BLOCK, BLOCK), F32)
    stri = jnp.zeros((LANES, BLOCK), F32)
    lane_rows = iota((LANES, BLOCK), 0)
    for h in range(heads):
        dec = decay_of(cums, cums_t, h, keep)
        v = scores * dec
        doh = masked(do, h, hdim)
        dxs = dxs + mm(v.astype(BF16), doh, 0, 0)
        dv = mm(doh, xs, 1, 1)
        ds = ds + dv * dec
        left = mm((dv * v).astype(BF16), before)
        line = jnp.sum(jnp.where(keep, left, 0.0), axis=0, keepdims=True)
        stri = jnp.where(lane_rows == h, line, stri)
    dsl = ds.astype(BF16)
    dxs_ref[...] = dxs
    dkq_ref[:, :ns] = mm(dsl, queries, 0, 0)
    dkq_ref[:, ns:] = mm(dsl, keys)
    str_ref[...] = stri.T


def back_kernel(hdim, kq_ref, xs_ref, cums_ref, dtb_ref, pre_ref, raw_ref, do_ref, dxs_ref, dkq_ref, str_ref,
                expc_ref, tail_ref, stepb_ref, stin_ref, cd_ref, s0_ref, dst_ref, rd_ref, inc_ref, skip_ref, cw_ref, rate_ref,
                dx_ref, ddt_ref, halo_ref, cg_ref, hg_ref, buf, rbuf):
    step_id = pl.program_id(0)
    ns = kq_ref.shape[1] // 2
    ch = xs_ref.shape[1]

    @pl.when(step_id == 0)
    def _():
        cg_ref[...] = jnp.zeros_like(cg_ref)
        hg_ref[...] = jnp.zeros_like(hg_ref)
        buf[0:PRE, :] = jnp.zeros_like(buf[0:PRE, :])
        buf[PRE + BLOCK :, :] = jnp.zeros_like(buf[PRE + BLOCK :, :])

    @pl.when(step_id > 0)
    def _():
        buf[PRE + BLOCK :, :] = buf[PRE : 2 * PRE, :]

    hmap = head_map(ch, hdim)
    keys, queries = kq_ref[:, :ns], kq_ref[:, ns:]
    cums = cums_ref[...]
    expc, tail = expc_ref[...].astype(F32), tail_ref[...].astype(F32)
    st = stin_ref[0] + cd_ref[0, 0:1, :] * s0_ref[...]
    dst = dst_ref[0] + rd_ref[0, 0:1, :] * inc_ref[...]
    st_low, dst_low = st.astype(BF16), dst.astype(BF16)
    do = do_ref[...].astype(F32)
    xs = xs_ref[...].astype(F32)
    carried = expc * mm(queries, st_low)
    dq = dkq_ref[:, ns:] + mm((do * expc).astype(BF16), st_low, 1, 1)
    dxs_up = tail * mm(keys, dst_low)
    dk = dkq_ref[:, :ns] + mm((xs * tail).astype(BF16), dst_low, 1, 1)
    dxs = dxs_ref[...] + dxs_up
    px = pre_ref[:, :ch]
    xc = px * sigmoid(px)
    dtb = dtb_ref[...]
    step = softplus(dtb)
    rate = rate_ref[0:1, :]
    dxc = stepb_ref[...].astype(F32) * dxs + skip_ref[0:1, :] * do
    dstep = mm_parts(xc * dxs, hmap, 1, 1, 1)
    arr = mm_parts(do * carried, hmap, 1, 1, 1)
    upd = mm_parts(xs * dxs_up, hmap, 1, 1, 1)
    rows, cols = iota((BLOCK, BLOCK), 0), iota((BLOCK, BLOCK), 1)
    through = mm_parts(jnp.sum(st * dst, axis=0, keepdims=True) * jnp.ones((8, 1), F32), hmap, 2, 1, 1)[0:1, :]
    dlogs = (
        str_ref[...]
        + mm((cols >= rows).astype(BF16), arr.astype(BF16))
        + mm((cols < rows).astype(BF16), upd.astype(BF16))
        + jnp.exp(cums[BLOCK - 1 : BLOCK, :]) * through
    )
    ddtb = (dstep + dlogs * rate) * sigmoid(dtb)
    ddt_ref[...] = ddtb.astype(BF16)
    dskip = mm_parts(do * xc, hmap, 1, 1, 1)
    hg_ref[0:1, :] += jnp.sum(ddtb, axis=0, keepdims=True)
    hg_ref[1:2, :] += jnp.sum(dlogs * step, axis=0, keepdims=True) * rate
    hg_ref[2:3, :] += jnp.sum(dskip, axis=0, keepdims=True)
    pre = pre_ref[...]
    sp = sigmoid(pre)
    dpre = jnp.concatenate([dxc, dk, dq], axis=1) * (sp * (1.0 + pre * (1.0 - sp)))
    buf[PRE : PRE + BLOCK, :] = dpre
    rbuf[...] = raw_ref[0].astype(F32)
    cg_ref[4:5, :] += jnp.sum(dpre, axis=0, keepdims=True)
    dx = jnp.zeros_like(dpre)
    halo = jnp.zeros((PRE, dpre.shape[1]), F32)
    for k in range(4):
        tap = cw_ref[k : k + 1, :]
        dx = dx + tap * buf[PRE + 3 - k : PRE + 3 - k + BLOCK, :]
        halo = halo + tap * buf[3 - k : 3 - k + PRE, :]
        cg_ref[k : k + 1, :] += jnp.sum(
            dpre * rbuf[PRE - 3 + k : PRE - 3 + k + BLOCK, :], axis=0, keepdims=True
        )
    dx_ref[...] = dx.astype(BF16)
    halo_ref[...] = halo


def rows_of(width, rows=BLOCK, rev=None):
    if rev is None:
        return pl.BlockSpec((rows, width), lambda i: (i, 0))
    return pl.BlockSpec((rows, width), lambda i: (rev - 1 - i, 0))


def slabs_of(a, b, rev=None):
    if rev is None:
        return pl.BlockSpec((1, a, b), lambda i: (i, 0, 0))
    return pl.BlockSpec((1, a, b), lambda i: (rev - 1 - i, 0, 0))


def fixed(a, b):
    return pl.BlockSpec((a, b), lambda i: (0, 0))


def sds(shape, dtype=F32):
    return jax.ShapeDtypeStruct(shape, dtype)


def shifted(values, axis, size, by):
    pairs = [(i, i + by) for i in range(size) if 0 <= i + by < size]
    return lax.ppermute(values, axis, pairs)


def gather_dp(values, dp, d_id):
    parts = [values] + [
        lax.ppermute(values, "dp", [(i, (i - j) % dp) for i in range(dp)]) for j in range(1, dp)
    ]
    if dp == 2:
        first = d_id == 0
        return jnp.stack([jnp.where(first, parts[0], parts[1]), jnp.where(first, parts[1], parts[0])])
    stacked = jnp.stack(parts)
    return jnp.take(stacked, (jnp.arange(dp) - d_id) % dp, axis=0)


def join_lanes(stacked):
    return jnp.concatenate([stacked[i] for i in range(stacked.shape[0])], axis=1)


def broadcast_last(values, axis, size):
    gap = size
    while gap > 1:
        pairs = [(i, i - gap // 2) for i in range(size - 1, -1, -gap)]
        values = values + lax.ppermute(values, axis, pairs)
        gap //= 2
    return values


def parts_dp(values, dp, d_id, axis=0):
    size = values.shape[axis] // dp

    def part(index):
        return lax.dynamic_slice_in_dim(values, index * size, size, axis)

    received = []
    for j in range(1, dp):
        sent = part((d_id + j) % dp).astype(BF16)
        received.append(lax.ppermute(sent, "dp", [(i, (i + j) % dp) for i in range(dp)]))
    return part(d_id), received


def scatter_dp(values, dp, d_id, axis=0):
    own, received = parts_dp(values, dp, d_id, axis)
    return own + sum(part.astype(F32) for part in received)


def shifted_ring(values, axis, size, by):
    return lax.ppermute(values, axis, [(i, (i + by) % size) for i in range(size)])


def others_over(values, axis, size):
    low = values.astype(BF16)
    return [shifted_ring(low, axis, size, j) for j in range(1, size)]


def in_order(parts, index, size):
    if size == 1:
        return parts[0]
    if size == 2:
        first = index == 0
        return jnp.concatenate(
            [jnp.where(first, parts[0], parts[1]), jnp.where(first, parts[1], parts[0])], axis=0
        )
    stacked = jnp.take(jnp.stack(parts), (index - jnp.arange(size)) % size, axis=0)
    return stacked.reshape((-1,) + parts[0].shape[1:])


def swap(values, axis, size, bit):
    return lax.ppermute(values, axis, [(i, i ^ bit) for i in range(size)])


def sum_over(values, axis, size, kind=F32):
    bit = 1
    while bit < size:
        values = values + swap(values.astype(kind), axis, size, bit).astype(F32)
        bit *= 2
    return values


def scatter_over(values, axis, size, index):
    bit = size // 2
    while bit:
        half = values.shape[0] // 2
        upper = (index & bit) != 0
        low, high = values[:half], values[half:]
        kept = jnp.where(upper, high, low)
        sent = jnp.where(upper, low, high).astype(BF16)
        values = kept + swap(sent, axis, size, bit).astype(F32)
        bit //= 2
    return values


def gather_chips(block, size):
    return jnp.concatenate([block] + [swap(block, "tp", size, mask) for mask in range(2, size, 2)], axis=0)


def gather_cores(blocks, size):
    return jnp.concatenate([blocks, swap(blocks, "tp", size, 1)], axis=0)


def source_block(block, index, size):
    mask = block ^ index
    return (mask >> 1) + (mask & 1) * (size // 2)


def scatter_cores(values, size, index):
    blocks = values.reshape((size // 2, 2, values.shape[0] // size) + values.shape[1:])
    side = index & 1
    own = lax.dynamic_index_in_dim(blocks, side, 1, keepdims=False)
    sent = lax.dynamic_index_in_dim(blocks, 1 - side, 1, keepdims=False).astype(BF16)
    return (own.astype(F32) + swap(sent, "tp", size, 1).astype(F32)).astype(BF16)


def scatter_chips(blocks, size, index):
    chip = index >> 1

    def block(mask):
        return lax.dynamic_index_in_dim(blocks, chip ^ mask, 0, keepdims=False)

    parts = [swap(block(mask), "tp", size, 2 * mask) for mask in range(1, size // 2)]
    return block(0), parts


def add_up(own, parts):
    return own.astype(F32) + sum(part.astype(F32) for part in parts)


def gather_over(values, axis, size, index):
    bit = 1
    while bit < size:
        other = swap(values, axis, size, bit)
        upper = (index & bit) != 0
        values = jnp.concatenate([jnp.where(upper, other, values), jnp.where(upper, values, other)], axis=0)
        bit *= 2
    return values


def carry_over(state, decay, axis, size, way):
    total = None
    for j in range(size - 1, 0, -1):
        part = shifted(state, axis, size, way * j)
        if total is None:
            total = part
        else:
            total = part + shifted(decay, axis, size, way * j)[0:1, :] * total
    return jnp.zeros_like(state) if total is None else total


def local(layer_input, norm_gain, in_weight, conv_weight, conv_bias, step_bias, rate_log, skip_gain,
          gate_gain, out_weight, cotangent):
    dp, cp, tp = lax.axis_size("dp"), lax.axis_size("cp"), lax.axis_size("tp")
    d_id, k_id = lax.axis_index("dp"), lax.axis_index("tp")
    own_rows, width = layer_input.shape
    inner = out_weight.shape[0] * dp
    conv_all = conv_weight.shape[1] * dp
    heads = step_bias.shape[0] * dp
    hdim = inner // heads
    ns = (conv_all - inner) // 2
    lh = heads // tp
    ch = inner // tp
    conv_ch = ch + 2 * ns
    tokens = own_rows * tp
    nb = tokens // BLOCK
    cols = ch + conv_ch + LANES
    taps = conv_weight.shape[0]

    def cut(values, start, size, axis=1):
        return lax.dynamic_slice_in_dim(values, start, size, axis)

    share = tp // dp
    in_t = in_weight.T
    thin = 16
    own_cols = jnp.concatenate(
        [
            cut(in_t, k_id * ch, ch, 0),
            cut(in_t, inner + k_id * ch, ch, 0),
            in_t[2 * inner : 2 * inner + 2 * ns],
            cut(in_t, inner + conv_all + k_id * lh, lh, 0),
            jnp.zeros((thin - lh, in_t.shape[1]), BF16),
        ],
        axis=0,
    )
    row_size = conv_all // dp

    def wide(values):
        return jnp.pad(values, ((0, 0), (0, row_size - values.shape[1])))

    heads_own = jnp.concatenate([step_bias, rate_log, skip_gain])[None]
    small = jnp.concatenate(
        [conv_weight, conv_bias[None], wide(norm_gain[None]), wide(gate_gain[None]), wide(heads_own)], axis=0
    )
    tail_rows = jnp.where(k_id == tp - 1, layer_input[-PRE:], jnp.zeros((PRE, width), BF16))
    small, own_cols, tail_rows = lax.optimization_barrier((small, own_cols, tail_rows))
    small = gather_dp(small, dp, d_id).astype(F32)
    w_parts = gather_dp(own_cols, dp, d_id)
    w_parts, out_weight = lax.optimization_barrier((w_parts, out_weight))
    w = jnp.pad(join_lanes(w_parts), ((0, LANES - thin), (0, 0)))
    x_all = lax.all_gather(layer_input, "tp", axis=0, tiled=True)
    halo = broadcast_last(shifted(tail_rows, "cp", cp, 1), "tp", tp)
    c_all = lax.all_gather(cotangent, "tp", axis=0, tiled=True)
    ow = gather_dp(cut(out_weight, (k_id % share) * ch, ch, 0), dp, d_id)
    ow = lax.dynamic_index_in_dim(ow, k_id // share, 0, keepdims=False)

    def row_of(index, size, at=0):
        return small[:, index, at : at + size].reshape(-1)

    taps_all = small[:, :taps].transpose(1, 0, 2).reshape(taps, conv_all)
    offset = row_of(taps, row_size)
    gain = row_of(taps + 1, width // dp)
    ggain = row_of(taps + 2, inner // dp)
    hs = heads // dp
    sbias, rlog, skip = (row_of(taps + 3, hs, i * hs) for i in range(3))

    def own_conv(values):
        return jnp.concatenate([cut(values, k_id * ch, ch), values[:, inner:]], axis=1)

    def pad8(values):
        return jnp.pad(values, ((0, 8 - values.shape[0]), (0, 0)))

    def head_row(values):
        return jnp.pad(cut(values[None], k_id * lh, lh), ((0, 7), (0, LANES - lh)))

    cw = pad8(own_conv(taps_all))
    cb = pad8(own_conv(offset[None]))
    sb = head_row(sbias)
    rate = head_row(-jnp.exp(rlog))
    skip_b = pad8(jnp.repeat(cut(skip[None], k_id * lh, lh), hdim, axis=1))
    own_gate = pad8(cut(ggain[None], k_id * ch, ch))
    gain_row = gain[None]

    def params(**kw):
        return pltpu.CompilerParams(dimension_semantics=("arbitrary",), **kw)

    def cost(weight):
        return pl.CostEstimate(flops=tokens * weight * ch, transcendentals=0, bytes_accessed=tokens * weight * 3600)

    normed, z, raw, pre, xs, kq, dtb, cums, expc, tail, stepb, stin, cd, fin, dtot = pl.pallas_call(
        lambda *refs: front_kernel(hdim, *refs),
        grid=(nb,),
        in_specs=[rows_of(width), fixed(PRE, width), fixed(1, width), fixed(cols, width), fixed(8, conv_ch),
                  fixed(8, conv_ch), fixed(8, LANES), fixed(8, LANES)],
        out_specs=[rows_of(width), rows_of(ch), slabs_of(PRE + BLOCK, conv_ch), rows_of(conv_ch), rows_of(ch),
                   rows_of(2 * ns), rows_of(LANES), rows_of(LANES), rows_of(ch), rows_of(ch), rows_of(ch),
                   slabs_of(ns, ch), slabs_of(8, ch), fixed(ns, ch), fixed(8, ch)],
        out_shape=[sds((tokens, width), BF16), sds((tokens, ch), BF16), sds((nb, PRE + BLOCK, conv_ch), BF16),
                   sds((tokens, conv_ch)), sds((tokens, ch), BF16), sds((tokens, 2 * ns), BF16),
                   sds((tokens, LANES)), sds((tokens, LANES)), sds((tokens, ch), BF16), sds((tokens, ch), BF16),
                   sds((tokens, ch), BF16), sds((nb, ns, ch)), sds((nb, 8, ch)),
                   sds((ns, ch)), sds((8, ch))],
        scratch_shapes=[pltpu.VMEM((PRE + BLOCK, conv_ch), F32), pltpu.VMEM((ns, ch), F32), pltpu.VMEM((8, ch), F32)],
        compiler_params=params(),
        name="front", cost_estimate=cost(12),
    )(x_all, halo, gain_row, w, cw, cb, sb, rate)

    s0 = carry_over(fin, dtot, "cp", cp, 1)

    inside = pl.pallas_call(
        lambda *refs: intra_kernel(hdim, lh, *refs),
        grid=(nb,),
        in_specs=[rows_of(2 * ns), rows_of(ch), rows_of(LANES)],
        out_specs=rows_of(ch),
        out_shape=sds((tokens, ch)),
        compiler_params=params(),
        name="intra", cost_estimate=cost(5),
    )(kq, xs, cums)

    mo, a, y, stat = pl.pallas_call(
        gate_kernel,
        grid=(nb,),
        in_specs=[rows_of(2 * ns), rows_of(ch), rows_of(ch), rows_of(ch), rows_of(ch), slabs_of(ns, ch),
                  slabs_of(8, ch), fixed(ns, ch), fixed(8, ch), fixed(8, ch), fixed(ch, width), rows_of(width)],
        out_specs=[rows_of(ch), rows_of(ch), rows_of(width), pl.BlockSpec((8, BLOCK), lambda i: (0, i))],
        out_shape=[sds((tokens, ch), BF16), sds((tokens, ch), BF16), sds((tokens, width), BF16), sds((8, tokens))],
        compiler_params=params(),
        name="gate", cost_estimate=cost(7),
    )(kq, expc, inside, pre, z, stin, cd, s0, skip_b, own_gate, ow, c_all)

    stats = sum_over(stat, "tp", tp)
    stats, y = lax.optimization_barrier((stats, y))

    do, dz, og, gz, gg, gain_z, dstl, rd, g0 = pl.pallas_call(
        lambda *refs: back_gate_kernel(inner, *refs),
        grid=(nb,),
        in_specs=[pl.BlockSpec((8, BLOCK), lambda i: (0, nb - 1 - i)), rows_of(ch, rev=nb), rows_of(ch, rev=nb),
                  rows_of(ch, rev=nb), rows_of(width, rev=nb), rows_of(width, rev=nb), fixed(8, ch),
                  rows_of(2 * ns, rev=nb), rows_of(ch, rev=nb), fixed(ch, width)],
        out_specs=[rows_of(ch, rev=nb), rows_of(ch, rev=nb), fixed(ch, width), fixed(ch, width), fixed(8, ch),
                   fixed(8, width),
                   slabs_of(ns, ch, nb), slabs_of(8, ch, nb), fixed(ns, ch)],
        out_shape=[sds((tokens, ch), BF16), sds((tokens, ch), BF16), sds((ch, width), BF16), sds((ch, width), BF16), sds((8, ch)),
                   sds((8, width)),
                   sds((nb, ns, ch)), sds((nb, 8, ch)), sds((ns, ch))],
        scratch_shapes=[pltpu.VMEM((ns, ch), F32), pltpu.VMEM((8, ch), F32), pltpu.VMEM((ch, width), F32),
                        pltpu.VMEM((ch, width), F32)],
        compiler_params=params(),
        name="back_gate", cost_estimate=cost(8),
    )(stats, mo, a, z, c_all, normed, own_gate, kq, expc, w)

    incoming = carry_over(g0, dtot, "cp", cp, -1)

    grp = dp * cp
    quarter = ch // grp
    c_id = lax.axis_index("cp")
    src = d_id * cp + c_id
    og_parts = []
    for j in range(grp):
        pairs = []
        for d in range(dp):
            for p in range(cp):
                for k in range(tp):
                    piece = (d * cp + p + j) % grp
                    slot = (k % share) * grp + piece
                    pairs.append(((d * cp + p) * tp + k, (k // share) * cp * tp + (slot % cp) * tp + slot // cp))
        send = cut(og, ((src + j) % grp) * quarter, quarter, 0)
        og_parts.append(lax.ppermute(send, ("dp", "cp", "tp"), pairs))
    gz_own, gz_parts = parts_dp(gz, dp, d_id, 1)
    y_sum = lax.psum_scatter(y, "tp", scatter_dimension=0, tiled=True)

    dxs, dkq, stri = pl.pallas_call(
        lambda *refs: back_intra_kernel(hdim, lh, *refs),
        grid=(nb,),
        in_specs=[rows_of(2 * ns), rows_of(ch), rows_of(LANES), rows_of(ch)],
        out_specs=[rows_of(ch), rows_of(2 * ns), rows_of(LANES)],
        out_shape=[sds((tokens, ch)), sds((tokens, 2 * ns)), sds((tokens, LANES))],
        compiler_params=params(),
        name="back_intra", cost_estimate=cost(7),
    )(kq, xs, cums, do)

    dxs, gz_parts, y_sum = lax.optimization_barrier((dxs, gz_parts, y_sum))
    gz_own = gz_own.astype(F32) + sum(part.astype(F32) for part in gz_parts)
    gz_others = others_over(gz_own, "cp", cp)

    dxbc, ddt, dhalo, cg, hg = pl.pallas_call(
        lambda *refs: back_kernel(hdim, *refs),
        grid=(nb,),
        in_specs=[rows_of(2 * ns, rev=nb), rows_of(ch, rev=nb), rows_of(LANES, rev=nb), rows_of(LANES, rev=nb),
                  rows_of(conv_ch, rev=nb), slabs_of(PRE + BLOCK, conv_ch, nb), rows_of(ch, rev=nb),
                  rows_of(ch, rev=nb), rows_of(2 * ns, rev=nb), rows_of(LANES, rev=nb), rows_of(ch, rev=nb),
                  rows_of(ch, rev=nb), rows_of(ch, rev=nb), slabs_of(ns, ch, nb),
                  slabs_of(8, ch, nb), fixed(ns, ch), slabs_of(ns, ch, nb), slabs_of(8, ch, nb), fixed(ns, ch),
                  fixed(8, ch), fixed(8, conv_ch), fixed(8, LANES)],
        out_specs=[rows_of(conv_ch, rev=nb), rows_of(LANES, rev=nb), fixed(PRE, conv_ch), fixed(8, conv_ch),
                   fixed(8, LANES)],
        out_shape=[sds((tokens, conv_ch), BF16), sds((tokens, LANES), BF16), sds((PRE, conv_ch)), sds((8, conv_ch)),
                   sds((8, LANES))],
        scratch_shapes=[pltpu.VMEM((2 * PRE + BLOCK, conv_ch), F32), pltpu.VMEM((PRE + BLOCK, conv_ch), F32)],
        compiler_params=params(),
        name="back", cost_estimate=cost(9),
    )(kq, xs, cums, dtb, pre, raw, do, dxs, dkq, stri, expc, tail, stepb, stin, cd, s0, dstl, rd, incoming, skip_b, cw, rate)

    def spread(values, total, start):
        return lax.dynamic_update_slice_in_dim(
            jnp.zeros(values.shape[:-1] + (total,), F32), values, start, values.ndim - 1
        )

    def full(values):
        return jnp.pad(values, ((0, 0), (0, conv_all - values.shape[1])))

    back_halo = shifted(dhalo, "cp", cp, -1)
    rest = jnp.concatenate([dxbc, ddt], axis=1)
    grad_main = mm(rest, normed, 0, 0)
    og_own = sum(part.astype(F32) for part in og_parts).astype(BF16)
    og_others = [shifted_ring(og_own, "cp", cp, j) for j in range(1, cp)]
    dn_main = mm(jnp.concatenate([dz, rest], axis=1), w).astype(BF16)
    back_halo, dn_main, grad_main, gz_others, og_others = lax.optimization_barrier(
        (back_halo, dn_main, grad_main, gz_others, og_others)
    )
    half = width // dp
    og_own = in_order([og_own] + og_others, c_id, cp)
    og_rows = og_own.shape[0]
    zg = jnp.concatenate(
        [add_up(gz_own, gz_others).astype(BF16)] + [og_own[:, j * half : (j + 1) * half] for j in range(dp)], axis=0
    )
    zg = lax.all_gather(zg, "tp", axis=0, tiled=False)

    halo_low = jnp.pad(back_halo.astype(BF16), ((0, 0), (0, LANES)))
    grad_rest = grad_main + mm(halo_low, normed[-PRE:], 0, 0)
    dn_fix = (dn_main[-PRE:].astype(F32) + mm(halo_low, w[ch:])).astype(BF16)
    dn_part = lax.dynamic_update_slice_in_dim(dn_main, dn_fix, tokens - PRE, 0)

    steps = [("tp", tp), ("dp", dp), ("cp", cp)]
    steps = [(axis, size, 1 << i) for axis, size in steps for i in range(size.bit_length() - 1)]

    def pack_next(values):
        if steps:
            axis, size, bit = steps.pop(0)
            values = values + swap(values, axis, size, bit)
        return values

    x_dt = jnp.concatenate([grad_rest[:ch], grad_rest[conv_ch : conv_ch + thin]], axis=0)
    x_own, x_parts = parts_dp(x_dt, dp, d_id, 1)
    dn_cores = scatter_cores(dn_part, tp, k_id)
    kq_cores = scatter_cores(grad_rest[ch:conv_ch], tp, k_id)
    x_parts, dn_cores, kq_cores, grad_rest = lax.optimization_barrier((x_parts, dn_cores, kq_cores, grad_rest))
    x_own = add_up(x_own, x_parts)
    x_others = others_over(x_own, "cp", cp)
    dn_own, dn_parts = scatter_chips(dn_cores, tp, k_id)
    kq_own, kq_parts = scatter_chips(kq_cores, tp, k_id)

    conv_part = jnp.concatenate([spread(cg[: taps + 1, :ch], inner, k_id * ch), cg[: taps + 1, ch:]], axis=1)
    gate_part = spread(gg[0:1] / own_gate[0:1], inner, k_id * ch)
    head_part = spread(hg[0:3, :lh], heads, k_id * lh).reshape(1, 3 * heads)
    gain_part = (gain_z[0:1] + jnp.sum(grad_rest * w[ch:].astype(F32), axis=0, keepdims=True)) / gain_row
    pack = jnp.concatenate([conv_part, full(gate_part), full(head_part), full(gain_part)], axis=0)
    pack = pack_next(pack)
    kq_parts, pack = lax.optimization_barrier((kq_parts, pack))
    kq_sum = scatter_dp(add_up(kq_own, kq_parts), dp, d_id, 1)
    pack = pack_next(pack)
    x_others, kq_sum, pack, dn_parts = lax.optimization_barrier((x_others, kq_sum, pack, dn_parts))
    xg = lax.all_gather(add_up(x_own, x_others).astype(BF16), "tp", axis=0, tiled=False)
    dn_sum = add_up(dn_own, dn_parts)
    kq_sum = sum_over(kq_sum, "cp", cp, BF16)
    pack = pack_next(pack)
    kq_sum, pack = lax.optimization_barrier((kq_sum, pack))
    kqg = gather_chips(kq_sum.astype(BF16), tp)
    pack = pack_next(pack)
    kqg, pack = lax.optimization_barrier((kqg, pack))
    kqg = gather_cores(kqg, tp)
    while steps:
        pack = pack_next(pack)
    place = source_block(jnp.arange(tp, dtype=jnp.int32), k_id, tp)
    kqg = jnp.take(kqg.reshape(tp, -1, kqg.shape[1]), place, axis=0).reshape(kqg.shape)

    y_own = y_sum.astype(F32)
    r_own = lax.rsqrt(cut(stats, k_id * own_rows, own_rows)[0] * (1.0 / inner) + EPS)[:, None]
    u = layer_input.astype(F32)
    layer_output = (u + y_own * r_own).astype(BF16)
    dn = dn_sum
    q = lax.rsqrt(jnp.mean(u * u, axis=-1, keepdims=True) + EPS)
    m = u * q
    dg = dn * gain_row
    input_grad = cotangent.astype(F32) + q * (dg - m * jnp.mean(dg * m, axis=-1, keepdims=True))

    proj_all = in_weight.shape[1]
    grid_shape = sds((proj_all, half))

    def widen_out_kernel(src_ref, out_ref):
        for j in range(dp):
            out_ref[:, j * half : (j + 1) * half] = src_ref[0, j * og_rows : (j + 1) * og_rows, :].astype(F32)

    def widen_pair_kernel(src_ref, *refs):
        out_ref = refs[-1]
        out_ref[:ch, :] = src_ref[0, :ch, :].astype(F32)
        out_ref[ch:, :] = src_ref[1, :ch, :].astype(F32)

    out_grad = pl.pallas_call(
        widen_out_kernel, grid=(tp,),
        in_specs=[pl.BlockSpec((1, ch, half), lambda i: (i, 1, 0))], out_specs=rows_of(width, og_rows),
        out_shape=sds((tp * og_rows, width)), compiler_params=params(), name="widen_out", cost_estimate=cost(6),
    )(zg)
    in_grad = pl.pallas_call(
        widen_pair_kernel, grid=(tp // 2,),
        in_specs=[pl.BlockSpec((2, ch, half), lambda i: (i, 0, 0))], out_specs=rows_of(half, 2 * ch),
        out_shape=grid_shape, compiler_params=params(), name="widen_z", cost_estimate=cost(5),
    )(zg)
    xg, in_grad, out_grad, input_grad = lax.optimization_barrier((xg, in_grad, out_grad, input_grad))

    in_grad = pl.pallas_call(
        widen_pair_kernel, grid=(tp // 2,),
        in_specs=[pl.BlockSpec((2, ch + thin, half), lambda i: (i, 0, 0)), pl.BlockSpec(memory_space=pl.ANY)],
        out_specs=pl.BlockSpec((2 * ch, half), lambda i: (i + tp // 2, 0)),
        out_shape=grid_shape, input_output_aliases={1: 0}, compiler_params=params(), name="widen_x", cost_estimate=cost(5),
    )(xg, in_grad)
    last = jnp.concatenate([kqg, xg[:, ch : ch + lh].reshape(heads, half)], axis=0)
    strip = last.shape[0]

    def last_kernel(src_ref, old_ref, out_ref, wide_ref, sem):
        wide_ref[...] = src_ref[...].astype(F32)
        copy = pltpu.make_async_copy(wide_ref, out_ref.at[pl.ds(proj_all - strip, strip)], sem)
        copy.start()
        copy.wait()

    in_grad = pl.pallas_call(
        last_kernel,
        in_specs=[pl.BlockSpec(memory_space=pltpu.VMEM), pl.BlockSpec(memory_space=pl.ANY)],
        out_specs=pl.BlockSpec(memory_space=pl.ANY),
        out_shape=grid_shape, input_output_aliases={1: 0},
        scratch_shapes=[pltpu.VMEM((strip, half), F32), pltpu.SemaphoreType.DMA], name="widen_kq",
    )(last, in_grad).T

    def own(values):
        size = values.shape[-1] // dp
        return lax.dynamic_slice_in_dim(values, d_id * size, size, values.ndim - 1)

    conv_own = own(pack[: taps + 1])
    head_own = own(pack[taps + 2, : 3 * heads].reshape(3, heads))
    gate_all = pack[taps + 1, :inner]
    return (
        layer_output,
        input_grad,
        own(pack[taps + 3, :width]),
        in_grad,
        conv_own[:taps],
        conv_own[taps],
        head_own[0],
        head_own[1],
        head_own[2],
        own(gate_all),
        out_grad,
    )


def solution(mesh):
    dp, group = mesh.devices.shape
    tp = 8 if group % 8 == 0 else group
    inner_mesh = Mesh(mesh.devices.reshape(dp, group // tp, tp), ("dp", "cp", "tp"))
    tok = P(("dp", "cp", "tp"), None)
    return jax.shard_map(
        local,
        mesh=inner_mesh,
        in_specs=(tok, P("dp"), P("dp", None), P(None, "dp"), P("dp"), P("dp"), P("dp"), P("dp"), P("dp"),
                  P("dp", None), tok),
        out_specs=(tok, tok, P("dp"), P("dp", None), P(None, "dp"), P("dp"), P("dp"), P("dp"), P("dp"), P("dp"),
                   P("dp", None)),
        check_vma=False,
    )
```

```python
import jax
import jax.numpy as jnp
from jax import lax
from jax.experimental import pallas as pl
from jax.experimental.pallas import tpu as pltpu
from jax.sharding import Mesh
from jax.sharding import PartitionSpec as P

BLOCK = 256
PRE = 16
LANES = 128
EPS = 1e-05
F32 = jnp.float32
BF16 = jnp.bfloat16


def mm(a, b, da=1, db=0):
    return lax.dot_general(a, b, (((da,), (db,)), ((), ())), preferred_element_type=F32)


def mm_parts(a, b, parts, da=1, db=0):
    total = None
    for _ in range(parts):
        high = a.astype(BF16)
        term = mm(high, b, da, db)
        total = term if total is None else total + term
        a = a - high.astype(F32)
    return total


def iota(shape, dim):
    return lax.broadcasted_iota(jnp.int32, shape, dim)


def head_map(channels, hdim):
    return (jnp.right_shift(iota((LANES, channels), 1), hdim.bit_length() - 1) == iota((LANES, channels), 0)).astype(BF16)


def unit(u):
    return u * lax.rsqrt(jnp.mean(u * u, axis=-1, keepdims=True) + EPS)


def sigmoid(v):
    return jax.nn.sigmoid(v)


def softplus(v):
    return jnp.maximum(v, 0.0) + jnp.log1p(jnp.exp(-jnp.abs(v)))


def masked(values, head, hdim):
    lanes = iota(values.shape, 1)
    own = (lanes >= head * hdim) & (lanes < (head + 1) * hdim)
    return jnp.where(own, values, jnp.zeros_like(values))


def front_kernel(hdim, x_ref, halo_ref, gain_ref, w_ref, cw_ref, cb_ref, sb_ref, rate_ref,
                 normed_ref, z_ref, raw_ref, pre_ref, xs_ref, kq_ref, dtb_ref, cums_ref, expc_ref, tail_ref, stepb_ref,
                 stin_ref, cd_ref, fin_ref, dtot_ref, buf, st, cd):
    step_id = pl.program_id(0)
    ch = z_ref.shape[1]
    conv_ch = pre_ref.shape[1]
    gain = gain_ref[...]

    @pl.when(step_id == 0)
    def _():
        hn = (unit(halo_ref[...].astype(F32)) * gain).astype(BF16)
        hp = mm(hn, w_ref[ch : ch + conv_ch, :], 1, 1)
        buf[0:PRE, :] = hp.astype(BF16).astype(F32)
        st[...] = jnp.zeros_like(st)
        cd[...] = jnp.ones_like(cd)

    @pl.when(step_id > 0)
    def _():
        buf[0:PRE, :] = buf[BLOCK : BLOCK + PRE, :]

    normed = (unit(x_ref[...].astype(F32)) * gain).astype(BF16)
    normed_ref[...] = normed
    proj = mm(normed, w_ref[...], 1, 1)
    z_ref[...] = proj[:, :ch].astype(BF16)
    buf[PRE : PRE + BLOCK, :] = proj[:, ch : ch + conv_ch].astype(BF16).astype(F32)
    raw_ref[0] = buf[...].astype(BF16)
    pre = cb_ref[0:1, :] + cw_ref[0:1, :] * buf[PRE - 3 : PRE - 3 + BLOCK, :]
    for k in range(1, 4):
        pre = pre + cw_ref[k : k + 1, :] * buf[PRE - 3 + k : PRE - 3 + k + BLOCK, :]
    pre_ref[...] = pre
    act = pre * sigmoid(pre)
    dtb = proj[:, ch + conv_ch :].astype(BF16).astype(F32) + sb_ref[0:1, :]
    dtb_ref[...] = dtb
    step = softplus(dtb)
    logs = step * rate_ref[0:1, :]
    upper = (iota((BLOCK, BLOCK), 0) <= iota((BLOCK, BLOCK), 1)).astype(BF16)
    cums = mm_parts(logs.T[:8, :], upper, 3)
    cums = jnp.concatenate([cums, jnp.zeros((LANES - 8, BLOCK), F32)], axis=0).T
    cums_ref[...] = cums
    hmap = head_map(ch, hdim)
    cums_b = mm_parts(cums, hmap, 3)
    step_b = mm_parts(step, hmap, 2)
    stepb_ref[...] = step_b.astype(BF16)
    xs = act[:, :ch] * step_b
    xs_ref[...] = xs.astype(BF16)
    kq = act[:, ch:].astype(BF16)
    kq_ref[...] = kq
    last = cums_b[BLOCK - 1 : BLOCK, :]
    tail = jnp.exp(last - cums_b)
    tail_ref[...] = tail.astype(BF16)
    expc_ref[...] = jnp.exp(cums_b).astype(BF16)
    update = mm(kq[:, : kq.shape[1] // 2], (xs * tail).astype(BF16), 0, 0)
    stin_ref[0] = st[...]
    cd_ref[0] = cd[...]
    decay = jnp.exp(last)
    st[...] = st[...] * decay + update
    cd[...] = cd[...] * decay
    fin_ref[...] = st[...]
    dtot_ref[...] = cd[...]


def decay_of(cums, cums_t, head, keep):
    spread = cums[:, head : head + 1] - cums_t[head : head + 1, :]
    return jnp.where(keep, jnp.exp(jnp.where(keep, spread, 0.0)), 0.0)


def intra_kernel(hdim, heads, kq_ref, xs_ref, cums_ref, out_ref):
    ns = kq_ref.shape[1] // 2
    keys, queries = kq_ref[:, :ns], kq_ref[:, ns:]
    scores = mm(queries, keys, 1, 1)
    cums = cums_ref[...]
    cums_t = cums.T
    xs = xs_ref[...]
    keep = iota((BLOCK, BLOCK), 0) >= iota((BLOCK, BLOCK), 1)
    total = jnp.zeros(xs.shape, F32)
    for h in range(heads):
        v = (scores * decay_of(cums, cums_t, h, keep)).astype(BF16)
        total = total + mm(v, masked(xs, h, hdim))
    out_ref[...] = total


def gate_kernel(kq_ref, expc_ref, ins_ref, pre_ref, z_ref, stin_ref, cd_ref, s0_ref,
                skip_ref, gain_ref, ow_ref, c_ref, mo_ref, a_ref, y_ref, stat_ref):
    ns = kq_ref.shape[1] // 2
    ch = ins_ref.shape[1]
    st = stin_ref[0] + cd_ref[0, 0:1, :] * s0_ref[...]
    carried = expc_ref[...].astype(F32) * mm(kq_ref[:, ns:], st.astype(BF16))
    px = pre_ref[...]
    xc = px * sigmoid(px)
    mo = (ins_ref[...] + carried + skip_ref[0:1, :] * xc).astype(BF16)
    mo_ref[...] = mo
    zf = z_ref[...].astype(F32)
    gated = mo.astype(F32) * (zf * sigmoid(zf))
    gain = gain_ref[0:1, :]
    y_ref[...] = mm((gated * gain).astype(BF16), ow_ref[...]).astype(BF16)
    a = mm(c_ref[...], ow_ref[...], 1, 1) * gain
    a_ref[...] = a.astype(BF16)
    sq = jnp.sum(gated * gated, axis=1, keepdims=True)
    pj = jnp.sum(gated * a, axis=1, keepdims=True)
    lanes = iota((BLOCK, LANES), 1)
    both = jnp.where(lanes == 0, sq, jnp.where(lanes == 1, pj, 0.0))
    stat_ref[...] = both.T[:8, :]


def back_gate_kernel(inner, stat_ref, mo_ref, a_ref, z_ref, c_ref, normed_ref, gain_ref, kq_ref, expc_ref, w_ref,
                     do_ref, dz_ref, og_ref, gz_ref, gg_ref, gs_ref, dst_ref, rd_ref, g0_ref, dst, rd, og, gz):
    step_id = pl.program_id(0)
    ns = kq_ref.shape[1] // 2

    @pl.when(step_id == 0)
    def _():
        dst[...] = jnp.zeros_like(dst)
        rd[...] = jnp.ones_like(rd)
        og[...] = jnp.zeros_like(og)
        gz[...] = jnp.zeros_like(gz)
        gg_ref[...] = jnp.zeros_like(gg_ref)

    stat = jnp.concatenate([stat_ref[...], jnp.zeros((LANES - 8, BLOCK), F32)], axis=0).T
    r = lax.rsqrt(stat[:, 0:1] * (1.0 / inner) + EPS)
    pj = stat[:, 1:2] * (1.0 / inner)
    mo = mo_ref[...].astype(F32)
    zf = z_ref[...].astype(F32)
    sz = sigmoid(zf)
    silu = zf * sz
    gated = mo * silu
    a = a_ref[...].astype(F32)
    n = gated * r
    gg_ref[0:1, :] += jnp.sum(a * n, axis=0, keepdims=True)
    dgated = r * (a - n * (r * pj))
    og[...] += mm((n * gain_ref[0:1, :]).astype(BF16), c_ref[...], 0, 0)
    do = (dgated * silu).astype(BF16)
    do_ref[...] = do
    dz = (dgated * mo * (sz * (1.0 + zf * (1.0 - sz)))).astype(BF16)
    dz_ref[...] = dz
    gz[...] += mm(dz, normed_ref[...], 0, 0)
    expc = expc_ref[...].astype(F32)
    dst_ref[0] = dst[...]
    rd_ref[0] = rd[...]
    decay = expc[BLOCK - 1 : BLOCK, :]
    carry = mm(kq_ref[:, ns:], (do.astype(F32) * expc).astype(BF16), 0, 0)
    dst[...] = dst[...] * decay + carry
    rd[...] = rd[...] * decay
    g0_ref[...] = dst[...]

    @pl.when(step_id == pl.num_programs(0) - 1)
    def _():
        og_ref[...] = og[...].astype(BF16)
        gz_ref[...] = gz[...].astype(BF16)
        gs_ref[...] = jnp.broadcast_to(
            jnp.sum(gz[...] * w_ref[...].astype(F32), axis=0, keepdims=True), gs_ref.shape
        )


def back_intra_kernel(hdim, heads, kq_ref, xs_ref, cums_ref, do_ref, dxs_ref, dkq_ref, str_ref):
    ns = kq_ref.shape[1] // 2
    keys, queries = kq_ref[:, :ns], kq_ref[:, ns:]
    scores = mm(queries, keys, 1, 1)
    cums = cums_ref[...]
    cums_t = cums.T
    xs, do = xs_ref[...], do_ref[...]
    rows, cols = iota((BLOCK, BLOCK), 0), iota((BLOCK, BLOCK), 1)
    keep = rows >= cols
    before = (rows < cols).astype(BF16)
    dxs = jnp.zeros(xs.shape, F32)
    ds = jnp.zeros((BLOCK, BLOCK), F32)
    stri = jnp.zeros((LANES, BLOCK), F32)
    lane_rows = iota((LANES, BLOCK), 0)
    for h in range(heads):
        dec = decay_of(cums, cums_t, h, keep)
        v = scores * dec
        doh = masked(do, h, hdim)
        dxs = dxs + mm(v.astype(BF16), doh, 0, 0)
        dv = mm(doh, xs, 1, 1)
        ds = ds + dv * dec
        left = mm((dv * v).astype(BF16), before)
        line = jnp.sum(jnp.where(keep, left, 0.0), axis=0, keepdims=True)
        stri = jnp.where(lane_rows == h, line, stri)
    dsl = ds.astype(BF16)
    dxs_ref[...] = dxs
    dkq_ref[:, :ns] = mm(dsl, queries, 0, 0)
    dkq_ref[:, ns:] = mm(dsl, keys)
    str_ref[...] = stri.T


def back_kernel(hdim, kq_ref, xs_ref, cums_ref, dtb_ref, pre_ref, raw_ref, do_ref, dxs_ref, dkq_ref, str_ref,
                expc_ref, tail_ref, stepb_ref, stin_ref, cd_ref, s0_ref, dst_ref, rd_ref, inc_ref, skip_ref, cw_ref, rate_ref,
                dx_ref, ddt_ref, halo_ref, cg_ref, hg_ref, buf, rbuf):
    step_id = pl.program_id(0)
    ns = kq_ref.shape[1] // 2
    ch = xs_ref.shape[1]

    @pl.when(step_id == 0)
    def _():
        cg_ref[...] = jnp.zeros_like(cg_ref)
        hg_ref[...] = jnp.zeros_like(hg_ref)
        buf[0:PRE, :] = jnp.zeros_like(buf[0:PRE, :])
        buf[PRE + BLOCK :, :] = jnp.zeros_like(buf[PRE + BLOCK :, :])

    @pl.when(step_id > 0)
    def _():
        buf[PRE + BLOCK :, :] = buf[PRE : 2 * PRE, :]

    hmap = head_map(ch, hdim)
    keys, queries = kq_ref[:, :ns], kq_ref[:, ns:]
    cums = cums_ref[...]
    expc, tail = expc_ref[...].astype(F32), tail_ref[...].astype(F32)
    st = stin_ref[0] + cd_ref[0, 0:1, :] * s0_ref[...]
    dst = dst_ref[0] + rd_ref[0, 0:1, :] * inc_ref[...]
    st_low, dst_low = st.astype(BF16), dst.astype(BF16)
    do = do_ref[...].astype(F32)
    xs = xs_ref[...].astype(F32)
    carried = expc * mm(queries, st_low)
    dq = dkq_ref[:, ns:] + mm((do * expc).astype(BF16), st_low, 1, 1)
    dxs_up = tail * mm(keys, dst_low)
    dk = dkq_ref[:, :ns] + mm((xs * tail).astype(BF16), dst_low, 1, 1)
    dxs = dxs_ref[...] + dxs_up
    px = pre_ref[:, :ch]
    xc = px * sigmoid(px)
    dtb = dtb_ref[...]
    step = softplus(dtb)
    rate = rate_ref[0:1, :]
    dxc = stepb_ref[...].astype(F32) * dxs + skip_ref[0:1, :] * do
    dstep = mm_parts(xc * dxs, hmap, 1, 1, 1)
    arr = mm_parts(do * carried, hmap, 1, 1, 1)
    upd = mm_parts(xs * dxs_up, hmap, 1, 1, 1)
    rows, cols = iota((BLOCK, BLOCK), 0), iota((BLOCK, BLOCK), 1)
    through = mm_parts(jnp.sum(st * dst, axis=0, keepdims=True) * jnp.ones((8, 1), F32), hmap, 2, 1, 1)[0:1, :]
    dlogs = (
        str_ref[...]
        + mm((cols >= rows).astype(BF16), arr.astype(BF16))
        + mm((cols < rows).astype(BF16), upd.astype(BF16))
        + jnp.exp(cums[BLOCK - 1 : BLOCK, :]) * through
    )
    ddtb = (dstep + dlogs * rate) * sigmoid(dtb)
    ddt_ref[...] = ddtb.astype(BF16)
    dskip = mm_parts(do * xc, hmap, 1, 1, 1)
    hg_ref[0:1, :] += jnp.sum(ddtb, axis=0, keepdims=True)
    hg_ref[1:2, :] += jnp.sum(dlogs * step, axis=0, keepdims=True) * rate
    hg_ref[2:3, :] += jnp.sum(dskip, axis=0, keepdims=True)
    pre = pre_ref[...]
    sp = sigmoid(pre)
    dpre = jnp.concatenate([dxc, dk, dq], axis=1) * (sp * (1.0 + pre * (1.0 - sp)))
    buf[PRE : PRE + BLOCK, :] = dpre
    rbuf[...] = raw_ref[0].astype(F32)
    cg_ref[4:5, :] += jnp.sum(dpre, axis=0, keepdims=True)
    dx = jnp.zeros_like(dpre)
    halo = jnp.zeros((PRE, dpre.shape[1]), F32)
    for k in range(4):
        tap = cw_ref[k : k + 1, :]
        dx = dx + tap * buf[PRE + 3 - k : PRE + 3 - k + BLOCK, :]
        halo = halo + tap * buf[3 - k : 3 - k + PRE, :]
        cg_ref[k : k + 1, :] += jnp.sum(
            dpre * rbuf[PRE - 3 + k : PRE - 3 + k + BLOCK, :], axis=0, keepdims=True
        )
    dx_ref[...] = dx.astype(BF16)
    halo_ref[...] = halo


def rows_of(width, rows=BLOCK, rev=None):
    if rev is None:
        return pl.BlockSpec((rows, width), lambda i: (i, 0))
    return pl.BlockSpec((rows, width), lambda i: (rev - 1 - i, 0))


def slabs_of(a, b, rev=None):
    if rev is None:
        return pl.BlockSpec((1, a, b), lambda i: (i, 0, 0))
    return pl.BlockSpec((1, a, b), lambda i: (rev - 1 - i, 0, 0))


def fixed(a, b):
    return pl.BlockSpec((a, b), lambda i: (0, 0))


def sds(shape, dtype=F32):
    return jax.ShapeDtypeStruct(shape, dtype)


def shifted(values, axis, size, by):
    pairs = [(i, i + by) for i in range(size) if 0 <= i + by < size]
    return lax.ppermute(values, axis, pairs)


def gather_dp(values, dp, d_id):
    parts = [values] + [
        lax.ppermute(values, "dp", [(i, (i - j) % dp) for i in range(dp)]) for j in range(1, dp)
    ]
    if dp == 2:
        first = d_id == 0
        return jnp.stack([jnp.where(first, parts[0], parts[1]), jnp.where(first, parts[1], parts[0])])
    stacked = jnp.stack(parts)
    return jnp.take(stacked, (jnp.arange(dp) - d_id) % dp, axis=0)


def join_lanes(stacked):
    return jnp.concatenate([stacked[i] for i in range(stacked.shape[0])], axis=1)


def broadcast_last(values, axis, size):
    gap = size
    while gap > 1:
        pairs = [(i, i - gap // 2) for i in range(size - 1, -1, -gap)]
        values = values + lax.ppermute(values, axis, pairs)
        gap //= 2
    return values


def parts_dp(values, dp, d_id, axis=0):
    size = values.shape[axis] // dp

    def part(index):
        return lax.dynamic_slice_in_dim(values, index * size, size, axis)

    received = []
    for j in range(1, dp):
        sent = part((d_id + j) % dp).astype(BF16)
        received.append(lax.ppermute(sent, "dp", [(i, (i + j) % dp) for i in range(dp)]))
    return part(d_id), received


def scatter_dp(values, dp, d_id, axis=0):
    own, received = parts_dp(values, dp, d_id, axis)
    return own + sum(part.astype(F32) for part in received)


def shifted_ring(values, axis, size, by):
    return lax.ppermute(values, axis, [(i, (i + by) % size) for i in range(size)])


def others_over(values, axis, size):
    low = values.astype(BF16)
    return [shifted_ring(low, axis, size, j) for j in range(1, size)]


def in_order(parts, index, size):
    if size == 1:
        return parts[0]
    if size == 2:
        first = index == 0
        return jnp.concatenate(
            [jnp.where(first, parts[0], parts[1]), jnp.where(first, parts[1], parts[0])], axis=0
        )
    stacked = jnp.take(jnp.stack(parts), (index - jnp.arange(size)) % size, axis=0)
    return stacked.reshape((-1,) + parts[0].shape[1:])


def swap(values, axis, size, bit):
    return lax.ppermute(values, axis, [(i, i ^ bit) for i in range(size)])


def sum_over(values, axis, size, kind=F32):
    bit = 1
    while bit < size:
        values = values + swap(values.astype(kind), axis, size, bit).astype(F32)
        bit *= 2
    return values


def scatter_over(values, axis, size, index):
    bit = size // 2
    while bit:
        half = values.shape[0] // 2
        upper = (index & bit) != 0
        low, high = values[:half], values[half:]
        kept = jnp.where(upper, high, low)
        sent = jnp.where(upper, low, high).astype(BF16)
        values = kept + swap(sent, axis, size, bit).astype(F32)
        bit //= 2
    return values


def gather_chips(block, size):
    return jnp.concatenate([block] + [swap(block, "tp", size, mask) for mask in range(2, size, 2)], axis=0)


def gather_cores(blocks, size):
    return jnp.concatenate([blocks, swap(blocks, "tp", size, 1)], axis=0)


def source_block(block, index, size):
    mask = block ^ index
    return (mask >> 1) + (mask & 1) * (size // 2)


def scatter_cores(values, size, index):
    blocks = values.reshape((size // 2, 2, values.shape[0] // size) + values.shape[1:])
    side = index & 1
    own = lax.dynamic_index_in_dim(blocks, side, 1, keepdims=False)
    sent = lax.dynamic_index_in_dim(blocks, 1 - side, 1, keepdims=False).astype(BF16)
    return (own.astype(F32) + swap(sent, "tp", size, 1).astype(F32)).astype(BF16)


def scatter_chips(blocks, size, index):
    chip = index >> 1

    def block(mask):
        return lax.dynamic_index_in_dim(blocks, chip ^ mask, 0, keepdims=False)

    parts = [swap(block(mask), "tp", size, 2 * mask) for mask in range(1, size // 2)]
    return block(0), parts


def add_up(own, parts):
    return own.astype(F32) + sum(part.astype(F32) for part in parts)


def gather_over(values, axis, size, index):
    bit = 1
    while bit < size:
        other = swap(values, axis, size, bit)
        upper = (index & bit) != 0
        values = jnp.concatenate([jnp.where(upper, other, values), jnp.where(upper, values, other)], axis=0)
        bit *= 2
    return values


def carry_over(state, decay, axis, size, way):
    total = None
    for j in range(size - 1, 0, -1):
        part = shifted(state.astype(BF16), axis, size, way * j).astype(F32)
        if total is None:
            total = part
        else:
            total = part + shifted(decay, axis, size, way * j)[0:1, :] * total
    return jnp.zeros_like(state) if total is None else total


def local(layer_input, norm_gain, in_weight, conv_weight, conv_bias, step_bias, rate_log, skip_gain,
          gate_gain, out_weight, cotangent):
    dp, cp, tp = lax.axis_size("dp"), lax.axis_size("cp"), lax.axis_size("tp")
    d_id, k_id = lax.axis_index("dp"), lax.axis_index("tp")
    own_rows, width = layer_input.shape
    inner = out_weight.shape[0] * dp
    conv_all = conv_weight.shape[1] * dp
    heads = step_bias.shape[0] * dp
    hdim = inner // heads
    ns = (conv_all - inner) // 2
    lh = heads // tp
    ch = inner // tp
    conv_ch = ch + 2 * ns
    tokens = own_rows * tp
    nb = tokens // BLOCK
    cols = ch + conv_ch + LANES
    taps = conv_weight.shape[0]

    def cut(values, start, size, axis=1):
        return lax.dynamic_slice_in_dim(values, start, size, axis)

    share = tp // dp
    in_t = in_weight.T
    thin = 16
    own_cols = jnp.concatenate(
        [
            cut(in_t, k_id * ch, ch, 0),
            cut(in_t, inner + k_id * ch, ch, 0),
            in_t[2 * inner : 2 * inner + 2 * ns],
            cut(in_t, inner + conv_all + k_id * lh, lh, 0),
            jnp.zeros((thin - lh, in_t.shape[1]), BF16),
        ],
        axis=0,
    )
    row_size = conv_all // dp

    def wide(values):
        return jnp.pad(values, ((0, 0), (0, row_size - values.shape[1])))

    heads_own = jnp.concatenate([step_bias, rate_log, skip_gain])[None]
    small = jnp.concatenate(
        [conv_weight, conv_bias[None], wide(norm_gain[None]), wide(gate_gain[None]), wide(heads_own)], axis=0
    )
    tail_rows = jnp.where(k_id == tp - 1, layer_input[-PRE:], jnp.zeros((PRE, width), BF16))
    small, own_cols, tail_rows = lax.optimization_barrier((small, own_cols, tail_rows))
    small = gather_dp(small, dp, d_id).astype(F32)
    w_parts = gather_dp(own_cols, dp, d_id)
    w_parts, out_weight = lax.optimization_barrier((w_parts, out_weight))
    w = jnp.pad(join_lanes(w_parts), ((0, LANES - thin), (0, 0)))
    x_all = lax.all_gather(layer_input, "tp", axis=0, tiled=True)
    halo = broadcast_last(shifted(tail_rows, "cp", cp, 1), "tp", tp)
    c_all = lax.all_gather(cotangent, "tp", axis=0, tiled=True)
    ow = cut(out_weight, (k_id % share) * ch, ch, 0)

    def row_of(index, size, at=0):
        return small[:, index, at : at + size].reshape(-1)

    taps_all = small[:, :taps].transpose(1, 0, 2).reshape(taps, conv_all)
    offset = row_of(taps, row_size)
    gain = row_of(taps + 1, width // dp)
    ggain = row_of(taps + 2, inner // dp)
    hs = heads // dp
    sbias, rlog, skip = (row_of(taps + 3, hs, i * hs) for i in range(3))

    def own_conv(values):
        return jnp.concatenate([cut(values, k_id * ch, ch), values[:, inner:]], axis=1)

    def pad8(values):
        return jnp.pad(values, ((0, 8 - values.shape[0]), (0, 0)))

    def head_row(values):
        return jnp.pad(cut(values[None], k_id * lh, lh), ((0, 7), (0, LANES - lh)))

    cw = pad8(own_conv(taps_all))
    cb = pad8(own_conv(offset[None]))
    sb = head_row(sbias)
    rate = head_row(-jnp.exp(rlog))
    skip_b = pad8(jnp.repeat(cut(skip[None], k_id * lh, lh), hdim, axis=1))
    own_gate = pad8(cut(ggain[None], k_id * ch, ch))
    gain_row = gain[None]

    def params(**kw):
        return pltpu.CompilerParams(dimension_semantics=("arbitrary",), **kw)

    def cost(weight):
        return pl.CostEstimate(flops=tokens * weight * ch, transcendentals=0, bytes_accessed=tokens * weight * 3600)

    normed, z, raw, pre, xs, kq, dtb, cums, expc, tail, stepb, stin, cd, fin, dtot = pl.pallas_call(
        lambda *refs: front_kernel(hdim, *refs),
        grid=(nb,),
        in_specs=[rows_of(width), fixed(PRE, width), fixed(1, width), fixed(cols, width), fixed(8, conv_ch),
                  fixed(8, conv_ch), fixed(8, LANES), fixed(8, LANES)],
        out_specs=[rows_of(width), rows_of(ch), slabs_of(PRE + BLOCK, conv_ch), rows_of(conv_ch), rows_of(ch),
                   rows_of(2 * ns), rows_of(LANES), rows_of(LANES), rows_of(ch), rows_of(ch), rows_of(ch),
                   slabs_of(ns, ch), slabs_of(8, ch), fixed(ns, ch), fixed(8, ch)],
        out_shape=[sds((tokens, width), BF16), sds((tokens, ch), BF16), sds((nb, PRE + BLOCK, conv_ch), BF16),
                   sds((tokens, conv_ch)), sds((tokens, ch), BF16), sds((tokens, 2 * ns), BF16),
                   sds((tokens, LANES)), sds((tokens, LANES)), sds((tokens, ch), BF16), sds((tokens, ch), BF16),
                   sds((tokens, ch), BF16), sds((nb, ns, ch)), sds((nb, 8, ch)),
                   sds((ns, ch)), sds((8, ch))],
        scratch_shapes=[pltpu.VMEM((PRE + BLOCK, conv_ch), F32), pltpu.VMEM((ns, ch), F32), pltpu.VMEM((8, ch), F32)],
        compiler_params=params(),
        name="front", cost_estimate=cost(12),
    )(x_all, halo, gain_row, w, cw, cb, sb, rate)

    s0 = carry_over(fin, dtot, "cp", cp, 1)
    cums, ow = lax.optimization_barrier((cums, ow))
    ow = lax.dynamic_index_in_dim(gather_dp(ow, dp, d_id), k_id // share, 0, keepdims=False)

    inside = pl.pallas_call(
        lambda *refs: intra_kernel(hdim, lh, *refs),
        grid=(nb,),
        in_specs=[rows_of(2 * ns), rows_of(ch), rows_of(LANES)],
        out_specs=rows_of(ch),
        out_shape=sds((tokens, ch)),
        compiler_params=params(),
        name="intra", cost_estimate=cost(5),
    )(kq, xs, cums)

    mo, a, y, stat = pl.pallas_call(
        gate_kernel,
        grid=(nb,),
        in_specs=[rows_of(2 * ns), rows_of(ch), rows_of(ch), rows_of(ch), rows_of(ch), slabs_of(ns, ch),
                  slabs_of(8, ch), fixed(ns, ch), fixed(8, ch), fixed(8, ch), fixed(ch, width), rows_of(width)],
        out_specs=[rows_of(ch), rows_of(ch), rows_of(width), pl.BlockSpec((8, BLOCK), lambda i: (0, i))],
        out_shape=[sds((tokens, ch), BF16), sds((tokens, ch), BF16), sds((tokens, width), BF16), sds((8, tokens))],
        compiler_params=params(),
        name="gate", cost_estimate=cost(7),
    )(kq, expc, inside, pre, z, stin, cd, s0, skip_b, own_gate, ow, c_all)

    stats = sum_over(stat, "tp", tp)
    stats, y = lax.optimization_barrier((stats, y))

    do, dz, og, gz, gg, gain_z, dstl, rd, g0 = pl.pallas_call(
        lambda *refs: back_gate_kernel(inner, *refs),
        grid=(nb,),
        in_specs=[pl.BlockSpec((8, BLOCK), lambda i: (0, nb - 1 - i)), rows_of(ch, rev=nb), rows_of(ch, rev=nb),
                  rows_of(ch, rev=nb), rows_of(width, rev=nb), rows_of(width, rev=nb), fixed(8, ch),
                  rows_of(2 * ns, rev=nb), rows_of(ch, rev=nb), fixed(ch, width)],
        out_specs=[rows_of(ch, rev=nb), rows_of(ch, rev=nb), fixed(ch, width), fixed(ch, width), fixed(8, ch),
                   fixed(8, width),
                   slabs_of(ns, ch, nb), slabs_of(8, ch, nb), fixed(ns, ch)],
        out_shape=[sds((tokens, ch), BF16), sds((tokens, ch), BF16), sds((ch, width), BF16), sds((ch, width), BF16), sds((8, ch)),
                   sds((8, width)),
                   sds((nb, ns, ch)), sds((nb, 8, ch)), sds((ns, ch))],
        scratch_shapes=[pltpu.VMEM((ns, ch), F32), pltpu.VMEM((8, ch), F32), pltpu.VMEM((ch, width), F32),
                        pltpu.VMEM((ch, width), F32)],
        compiler_params=params(),
        name="back_gate", cost_estimate=cost(8),
    )(stats, mo, a, z, c_all, normed, own_gate, kq, expc, w)

    incoming = carry_over(g0, dtot, "cp", cp, -1)

    grp = dp * cp
    quarter = ch // grp
    c_id = lax.axis_index("cp")
    src = d_id * cp + c_id
    gz_own, gz_parts = parts_dp(gz, dp, d_id, 1)
    y_sum = lax.psum_scatter(y, "tp", scatter_dimension=0, tiled=True)

    dxs, dkq, stri = pl.pallas_call(
        lambda *refs: back_intra_kernel(hdim, lh, *refs),
        grid=(nb,),
        in_specs=[rows_of(2 * ns), rows_of(ch), rows_of(LANES), rows_of(ch)],
        out_specs=[rows_of(ch), rows_of(2 * ns), rows_of(LANES)],
        out_shape=[sds((tokens, ch)), sds((tokens, 2 * ns)), sds((tokens, LANES))],
        compiler_params=params(),
        name="back_intra", cost_estimate=cost(7),
    )(kq, xs, cums, do)

    dxs, gz_parts = lax.optimization_barrier((dxs, gz_parts))
    gz_own = gz_own.astype(F32) + sum(part.astype(F32) for part in gz_parts)
    gz_others = others_over(gz_own, "cp", cp)
    dxbc, ddt, dhalo, cg, hg = pl.pallas_call(
        lambda *refs: back_kernel(hdim, *refs),
        grid=(nb,),
        in_specs=[rows_of(2 * ns, rev=nb), rows_of(ch, rev=nb), rows_of(LANES, rev=nb), rows_of(LANES, rev=nb),
                  rows_of(conv_ch, rev=nb), slabs_of(PRE + BLOCK, conv_ch, nb), rows_of(ch, rev=nb),
                  rows_of(ch, rev=nb), rows_of(2 * ns, rev=nb), rows_of(LANES, rev=nb), rows_of(ch, rev=nb),
                  rows_of(ch, rev=nb), rows_of(ch, rev=nb), slabs_of(ns, ch, nb),
                  slabs_of(8, ch, nb), fixed(ns, ch), slabs_of(ns, ch, nb), slabs_of(8, ch, nb), fixed(ns, ch),
                  fixed(8, ch), fixed(8, conv_ch), fixed(8, LANES)],
        out_specs=[rows_of(conv_ch, rev=nb), rows_of(LANES, rev=nb), fixed(PRE, conv_ch), fixed(8, conv_ch),
                   fixed(8, LANES)],
        out_shape=[sds((tokens, conv_ch), BF16), sds((tokens, LANES), BF16), sds((PRE, conv_ch)), sds((8, conv_ch)),
                   sds((8, LANES))],
        scratch_shapes=[pltpu.VMEM((2 * PRE + BLOCK, conv_ch), F32), pltpu.VMEM((PRE + BLOCK, conv_ch), F32)],
        compiler_params=params(),
        name="back", cost_estimate=cost(9),
    )(kq, xs, cums, dtb, pre, raw, do, dxs, dkq, stri, expc, tail, stepb, stin, cd, s0, dstl, rd, incoming, skip_b, cw, rate)

    def spread(values, total, start):
        return lax.dynamic_update_slice_in_dim(
            jnp.zeros(values.shape[:-1] + (total,), F32), values, start, values.ndim - 1
        )

    def full(values):
        return jnp.pad(values, ((0, 0), (0, conv_all - values.shape[1])))

    back_halo = shifted(dhalo, "cp", cp, -1)
    dxbc, y_sum = lax.optimization_barrier((dxbc, y_sum))
    rest = jnp.concatenate([dxbc, ddt], axis=1)
    grad_main = mm(rest, normed, 0, 0)
    back_halo, grad_main, gz_others = lax.optimization_barrier((back_halo, grad_main, gz_others))
    zg = lax.all_gather(add_up(gz_own, gz_others).astype(BF16), "tp", axis=0, tiled=False)

    halo_low = jnp.pad(back_halo.astype(BF16), ((0, 0), (0, LANES)))
    grad_rest = grad_main + mm(halo_low, normed[-PRE:], 0, 0)
    x_dt = jnp.concatenate([grad_rest[:ch], grad_rest[conv_ch : conv_ch + thin]], axis=0)
    x_own, x_parts = parts_dp(x_dt, dp, d_id, 1)
    grad_rest, rest, x_own = lax.optimization_barrier((grad_rest, rest, x_own))
    dn_main = mm(jnp.concatenate([dz, rest], axis=1), w).astype(BF16)
    dn_fix = (dn_main[-PRE:].astype(F32) + mm(halo_low, w[ch:])).astype(BF16)
    dn_part = lax.dynamic_update_slice_in_dim(dn_main, dn_fix, tokens - PRE, 0)
    dn_part, x_parts = lax.optimization_barrier((dn_part, x_parts))
    x_own = add_up(x_own, x_parts)
    x_own, dn_part, grad_rest, og = lax.optimization_barrier((x_own, dn_part, grad_rest, og))
    x_others = others_over(x_own, "cp", cp)
    og_parts = []
    for j in range(grp):
        pairs = []
        for d in range(dp):
            for p in range(cp):
                for k in range(tp):
                    piece = (d * cp + p + j) % grp
                    slot = (k % share) * grp + piece
                    pairs.append(((d * cp + p) * tp + k, (k // share) * cp * tp + (slot % cp) * tp + slot // cp))
        send = cut(og, ((src + j) % grp) * quarter, quarter, 0)
        og_parts.append(lax.ppermute(send, ("dp", "cp", "tp"), pairs))
    steps = [("tp", tp), ("dp", dp), ("cp", cp)]
    steps = [(axis, size, 1 << i) for axis, size in steps for i in range(size.bit_length() - 1)]

    def pack_next(values):
        if steps:
            axis, size, bit = steps.pop(0)
            values = values + swap(values, axis, size, bit)
        return values

    dn_cores = scatter_cores(dn_part, tp, k_id)
    kq_cores = scatter_cores(grad_rest[ch:conv_ch], tp, k_id)
    dn_cores, kq_cores, grad_rest, zg, og_parts = lax.optimization_barrier(
        (dn_cores, kq_cores, grad_rest, zg, og_parts)
    )
    half = width // dp
    og_own = sum(part.astype(F32) for part in og_parts).astype(BF16)
    og_others = [shifted_ring(og_own, "cp", cp, j) for j in range(1, cp)]
    dn_own, dn_parts = scatter_chips(dn_cores, tp, k_id)
    kq_own, kq_parts = scatter_chips(kq_cores, tp, k_id)

    conv_part = jnp.concatenate([spread(cg[: taps + 1, :ch], inner, k_id * ch), cg[: taps + 1, ch:]], axis=1)
    gate_part = spread(gg[0:1] / own_gate[0:1], inner, k_id * ch)
    head_part = spread(hg[0:3, :lh], heads, k_id * lh).reshape(1, 3 * heads)
    gain_part = (gain_z[0:1] + jnp.sum(grad_rest * w[ch:].astype(F32), axis=0, keepdims=True)) / gain_row
    pack = jnp.concatenate([conv_part, full(gate_part), full(head_part), full(gain_part)], axis=0)
    pack = pack_next(pack)
    kq_parts, pack = lax.optimization_barrier((kq_parts, pack))
    kq_sum = scatter_dp(add_up(kq_own, kq_parts), dp, d_id, 1)
    pack = pack_next(pack)
    x_others, kq_sum, pack, og_others = lax.optimization_barrier((x_others, kq_sum, pack, og_others))
    og_own = in_order([og_own] + og_others, c_id, cp)
    og_rows = og_own.shape[0]
    x_own = add_up(x_own, x_others).astype(BF16)
    xg = jnp.concatenate(
        [x_own[:ch]] + [og_own[:, j * half : (j + 1) * half] for j in range(dp)] + [x_own[ch:]], axis=0
    )
    xg = lax.all_gather(xg, "tp", axis=0, tiled=False)
    dn_parts, kq_sum = lax.optimization_barrier((dn_parts, kq_sum))
    dn_sum = add_up(dn_own, dn_parts)
    kq_sum = sum_over(kq_sum, "cp", cp, BF16)
    pack = pack_next(pack)
    proj_all = in_weight.shape[1]
    grid_shape = sds((proj_all, half))

    def widen_out_kernel(src_ref, out_ref):
        for j in range(dp):
            out_ref[:, j * half : (j + 1) * half] = src_ref[0, j * og_rows : (j + 1) * og_rows, :].astype(F32)

    def widen_pair_kernel(src_ref, *refs):
        out_ref = refs[-1]
        out_ref[:ch, :] = src_ref[0, :ch, :].astype(F32)
        out_ref[ch:, :] = src_ref[1, :ch, :].astype(F32)

    in_grad = pl.pallas_call(
        widen_pair_kernel, grid=(tp // 2,),
        in_specs=[pl.BlockSpec((2, ch, half), lambda i: (i, 0, 0))], out_specs=rows_of(half, 2 * ch),
        out_shape=grid_shape, compiler_params=params(), name="widen_z", cost_estimate=cost(5),
    )(zg)
    kq_sum, pack, in_grad = lax.optimization_barrier((kq_sum, pack, in_grad))
    kqg = gather_chips(kq_sum.astype(BF16), tp)
    pack = pack_next(pack)
    kqg, pack = lax.optimization_barrier((kqg, pack))
    kqg = gather_cores(kqg, tp)
    while steps:
        pack = pack_next(pack)
    place = source_block(jnp.arange(tp, dtype=jnp.int32), k_id, tp)
    kqg = jnp.take(kqg.reshape(tp, -1, kqg.shape[1]), place, axis=0).reshape(kqg.shape)

    y_own = y_sum.astype(F32)
    r_own = lax.rsqrt(cut(stats, k_id * own_rows, own_rows)[0] * (1.0 / inner) + EPS)[:, None]
    u = layer_input.astype(F32)
    layer_output = (u + y_own * r_own).astype(BF16)
    dn = dn_sum
    q = lax.rsqrt(jnp.mean(u * u, axis=-1, keepdims=True) + EPS)
    m = u * q
    dg = dn * gain_row
    input_grad = cotangent.astype(F32) + q * (dg - m * jnp.mean(dg * m, axis=-1, keepdims=True))

    in_grad = pl.pallas_call(
        widen_pair_kernel, grid=(tp // 2,),
        in_specs=[pl.BlockSpec((2, ch, half), lambda i: (i, 0, 0)), pl.BlockSpec(memory_space=pl.ANY)],
        out_specs=pl.BlockSpec((2 * ch, half), lambda i: (i + tp // 2, 0)),
        out_shape=grid_shape, input_output_aliases={1: 0}, compiler_params=params(), name="widen_x", cost_estimate=cost(5),
    )(xg, in_grad)
    last = jnp.concatenate([kqg, xg[:, 2 * ch : 2 * ch + lh].reshape(heads, half)], axis=0)
    strip = last.shape[0]

    def last_kernel(src_ref, old_ref, out_ref, wide_ref, sem):
        wide_ref[...] = src_ref[...].astype(F32)
        copy = pltpu.make_async_copy(wide_ref, out_ref.at[pl.ds(proj_all - strip, strip)], sem)
        copy.start()
        copy.wait()

    in_grad = pl.pallas_call(
        last_kernel,
        in_specs=[pl.BlockSpec(memory_space=pltpu.VMEM), pl.BlockSpec(memory_space=pl.ANY)],
        out_specs=pl.BlockSpec(memory_space=pl.ANY),
        out_shape=grid_shape, input_output_aliases={1: 0},
        scratch_shapes=[pltpu.VMEM((strip, half), F32), pltpu.SemaphoreType.DMA], name="widen_kq",
    )(last, in_grad).T
    out_grad = pl.pallas_call(
        widen_out_kernel, grid=(tp,),
        in_specs=[pl.BlockSpec((1, ch, half), lambda i: (i, 1, 0))], out_specs=rows_of(width, og_rows),
        out_shape=sds((tp * og_rows, width)), compiler_params=params(), name="widen_out", cost_estimate=cost(6),
    )(xg)


    def own(values):
        size = values.shape[-1] // dp
        return lax.dynamic_slice_in_dim(values, d_id * size, size, values.ndim - 1)

    conv_own = own(pack[: taps + 1])
    head_own = own(pack[taps + 2, : 3 * heads].reshape(3, heads))
    gate_all = pack[taps + 1, :inner]
    return (
        layer_output,
        input_grad,
        own(pack[taps + 3, :width]),
        in_grad,
        conv_own[:taps],
        conv_own[taps],
        head_own[0],
        head_own[1],
        head_own[2],
        own(gate_all),
        out_grad,
    )


def solution(mesh):
    dp, group = mesh.devices.shape
    tp = 8 if group % 8 == 0 else group
    inner_mesh = Mesh(mesh.devices.reshape(dp, group // tp, tp), ("dp", "cp", "tp"))
    tok = P(("dp", "cp", "tp"), None)
    return jax.shard_map(
        local,
        mesh=inner_mesh,
        in_specs=(tok, P("dp"), P("dp", None), P(None, "dp"), P("dp"), P("dp"), P("dp"), P("dp"), P("dp"),
                  P("dp", None), tok),
        out_specs=(tok, tok, P("dp"), P("dp", None), P(None, "dp"), P("dp"), P("dp"), P("dp"), P("dp"), P("dp"),
                   P("dp", None)),
        check_vma=False,
    )
```
